32 devices in a mesh: run: 2 (over y), team: 4 (over x, core), ma: 4 (over z).
Axes of the slice: x: 2, y: 2, z: 4, core: 2. Of those that a mesh axis runs over, the one named last changes fastest.
Arguments:
- section: bfloat16 [8, 2, 3, 24, 2, 32896], P(('run', 'team'), None, None, None, None, 'ma'), parts along dimension 0, may hold values from -6 to 6
- start: float32 [8, 2, 3, 24, 2, 32896], P(('run', 'team'), None, None, None, None, 'ma'), parts along dimension 0, may hold values from -6 to 6
- velocity: bfloat16 [768, 3, 24, 768], P(('run', 'ma'), None, 'team'), parts along dimension 0, may hold values from -6 to 6
- pair_list: int32 [128], P('ma'), may hold values from 0 to 127, each once
- wavenumber: int32 [4], P('team'), may hold values from 1 to 23
Outputs:
- updated: float32 [8, 2, 3, 24, 2, 32896], P(('run', 'team'), None, None, None, None, 'ma'), parts along dimension 0
The draws below stay inside these ranges and needn't reach their ends.
There are 2 independent parts, one for each index of `run`. The reference program is written for one: setup_inputs(seed, part) draws one part's arguments, and reference() takes and returns one part's arrays. A program takes and returns all parts, laid end to end along the dimension named above; an argument that names none is the same for every part. Nothing has to cross between parts.
Inputs may be any that keep to these rules, and one draw needn't show every extreme that they name: Block q of the rows holds orders pair_list[q] and 255 - pair_list[q]; each value appears once.
All inputs are finite; a program needn't handle non-finite values.
Results may differ from the reference program's by a relative error of at most 0.0078.
Values may be sent and summed in bfloat16 or wider, within the bound.
No kernel may reach another device: no remote copies, remote signals or barrier semaphores. Data moves between devices by JAX's collectives and lax.ppermute only.
A program may use at most 320 MiB of HBM per device.

```python
import math
import jax
import jax.numpy as jnp
from jax import lax

NM = 256
NLAT = 384
NLON = 768
LEV = 24
TESTS = 2
TEAMS = 4
ROWS = 32896


def with_ends(values, key, low, top_value):
    longest = values.shape.index(max(values.shape))
    spots = []
    for shift in (0, 1):
        where = [jax.random.randint(jax.random.fold_in(key, axis), (), 0, length) for axis, length in enumerate(values.shape)]
        where[longest] = (where[longest] + shift) % values.shape[longest]
        spots.append(tuple(where))
    return values.at[spots[0]].set(low).at[spots[1]].set(top_value)


def block_levels(rng, shape, cuts, least, high):
    gain = 1.0
    for dim, shards_of in cuts:
        steps = jax.random.uniform(jax.random.fold_in(jax.random.fold_in(rng, 6), dim), (shards_of,), jnp.float32, least / len(cuts), high / len(cuts))
        gain = gain * jnp.repeat(jnp.exp(steps), shape[dim] // shards_of).reshape((-1,) + (1,) * (len(shape) - 1 - dim))
    return gain


def gaussian(own_key, extent, scale, most, split=(), held_as=jnp.bfloat16):
    factor_of = block_levels(own_key, extent, split, -0.22, 0.18) if split else 1.0
    drawn = jax.random.normal(own_key, extent, jnp.float32) * scale * factor_of
    return jnp.minimum(jnp.maximum(drawn, -most), most).astype(held_as)


def setup_inputs(seed: int = 0, part: int = 0) -> dict:
    key_list = jax.random.split(jax.random.key(seed), 6)
    part_splits = jax.random.split(jax.random.fold_in(key_list[5], part), 6)
    return {
        "section": gaussian(part_splits[0], (TEAMS, TESTS, 3, LEV, 2, ROWS), 1.0, 6.0, ((0, 4), (5, 4))),
        "start": gaussian(part_splits[1], (TEAMS, TESTS, 3, LEV, 2, ROWS), 1.0, 6.0, ((0, 4), (5, 4)), jnp.float32),
        "velocity": gaussian(part_splits[2], (NLAT, 3, LEV, NLON), 1.0, 6.0, ((0, 4), (2, 4))),
        "pair_list": jax.random.permutation(key_list[3], NM // 2).astype(jnp.int32),
        "wavenumber": with_ends(jax.random.randint(key_list[4], (TEAMS,), 1, LEV), jax.random.fold_in(key_list[4], 1), 1, LEV - 1).astype(jnp.int32),
    }


grid_scale = 1.0 / 64.0
anchor_gain = 64.0 * math.sqrt(4.0 * math.pi)
quadrature_gain = 64.0
diffusion = 7e-06
step_weight = 2.0
row_block = 16

def seed_values(order_real, order_count, sine_theta):
    factor_index = jnp.arange(1, order_count, dtype=jnp.float32)
    factor_log = jnp.log((2.0 * factor_index - 1.0) / (2.0 * factor_index))
    partial_log = lax.optimization_barrier(jnp.sum(jnp.where(factor_index[None, :] <= order_real[:, None], factor_log[None, :], 0.0), axis=1))
    seed_log = 0.5 * (jnp.log((2.0 * order_real + 1.0) / (4.0 * jnp.pi)) + partial_log)
    return jnp.exp(seed_log[:, None] + order_real[:, None] * jnp.log(sine_theta)[None, :])

def pair_table(pair_ids, order_count, lat_count):
    pair_count = pair_ids.shape[0]
    pair_ids = pair_ids.astype(jnp.int32)
    order_low = pair_ids.astype(jnp.float32)
    order_high = (order_count - 1 - pair_ids).astype(jnp.float32)
    colatitude = jnp.pi * (jnp.arange(lat_count, dtype=jnp.float32) + 0.5) / lat_count
    cosine = jnp.cos(colatitude)
    sine_theta = jnp.sin(colatitude)
    seed_low = seed_values(order_low, order_count, sine_theta)
    seed_high = seed_values(order_high, order_count, sine_theta)
    switch_row = (order_count - pair_ids).astype(jnp.int32)

    def one_row(state_pair, row_id):
        latest, before = state_pair
        in_low = row_id < switch_row
        degree = jnp.where(in_low, pair_ids + row_id, row_id - 1).astype(jnp.int32)
        order_real = jnp.where(in_low, order_low, order_high)
        degree_real = degree.astype(jnp.float32)
        active = degree_real > order_real
        divisor = jnp.where(active, degree_real * degree_real - order_real * order_real, 1.0)
        upper = jnp.sqrt(jnp.maximum(4.0 * degree_real * degree_real - 1.0, 0.0) / divisor)
        lower_num = ((degree_real - 1.0) * (degree_real - 1.0) - order_real * order_real) * (2.0 * degree_real + 1.0)
        lower = jnp.sqrt(jnp.maximum(lower_num, 0.0) / (divisor * jnp.maximum(2.0 * degree_real - 3.0, 1.0)))
        recurred = upper[:, None] * cosine[None, :] * latest - lower[:, None] * before
        is_seed = (row_id == 0) | (row_id == switch_row)
        seeded = jnp.where(in_low[:, None], seed_low, seed_high)
        current = jnp.where(is_seed[:, None], seeded, jnp.where(active[:, None], recurred, 0.0))
        return ((current, latest), current)

    def block_rows(state_pair, first_row):
        produced = []
        for offset in range(row_block):
            state_pair, current = one_row(state_pair, first_row + offset)
            produced.append(current)
        return (state_pair, jnp.stack(produced))
    turns = -(-(order_count + 1) // row_block)
    blank_rows = jnp.zeros((pair_count, lat_count), jnp.float32)
    firsts = jnp.arange(turns, dtype=jnp.int32) * row_block
    _, values = lax.scan(block_rows, (blank_rows, blank_rows), firsts)
    leg_table = values.reshape(turns * row_block, pair_count, lat_count)[:order_count + 1]
    row_index = jnp.arange(order_count + 1, dtype=jnp.int32)
    first_half = row_index[None, :] < (order_count - pair_ids)[:, None]
    degree = jnp.where(first_half, pair_ids[:, None] + row_index[None, :], row_index[None, :] - 1).astype(jnp.int32)
    return (leg_table, first_half, degree)

def wave_table(order_list, lon_count):
    longitude = jnp.arange(lon_count, dtype=jnp.int32)
    phase_index = order_list[:, None] * longitude[None, :] % lon_count
    angle_rad = 2.0 * jnp.pi / lon_count * phase_index.astype(jnp.float32)
    return jnp.stack([jnp.cos(angle_rad), jnp.sin(angle_rad)])

def lat_weights(latitudes, lat_count):
    colatitude = jnp.pi * (latitudes.astype(jnp.float32) + 0.5) / lat_count
    return quadrature_gain * (jnp.pi / lat_count) * jnp.sin(colatitude)

def test_field(wave_index, test_count, levels):
    component = jnp.arange(3, dtype=jnp.int32)
    test_ids = jnp.arange(test_count, dtype=jnp.int32)
    level_ids = jnp.arange(levels, dtype=jnp.float32)
    aligned = (component[None, :] == test_ids[:, None]).astype(jnp.float32)
    profile = jnp.cos(jnp.pi * wave_index.astype(jnp.float32) * (level_ids + 0.5) / levels)
    return anchor_gain * aligned[:, :, None] * profile[None, None, :]

def cross_field(motion, magnetic, along):
    return jnp.roll(motion, -1, along) * jnp.roll(magnetic, -2, along) - jnp.roll(motion, -2, along) * jnp.roll(magnetic, -1, along)

def reference(section, start, velocity, pair_list, wavenumber):
    pair_count = pair_list.shape[0]
    leg_table, first_half, degree = pair_table(pair_list, NM, NLAT)
    legendre = leg_table.astype(jnp.bfloat16).astype(jnp.float32)
    selectors = jnp.stack([first_half, jnp.logical_not(first_half)], axis=1)
    masks_low = selectors.astype(jnp.bfloat16)
    masks_real = selectors.astype(jnp.float32)
    anchor = (pair_list == 0)[:, None] & (jnp.arange(NM + 1) == 0)[None, :]
    anchor_rows = anchor.reshape(-1).astype(jnp.float32)
    part_pick = jnp.array([1.0, 0.0], jnp.float32)
    order_list = jnp.stack([pair_list, NM - 1 - pair_list], axis=1).reshape(-1).astype(jnp.int32)
    waves = wave_table(order_list, NLON)
    inverse_table = (waves * grid_scale).astype(jnp.bfloat16).astype(jnp.float32)
    forward_table = (waves * (2.0 * jnp.pi / NLON)).astype(jnp.bfloat16).astype(jnp.float32)
    weights = lat_weights(jnp.arange(NLAT, dtype=jnp.int32), NLAT)
    spread = (degree * (degree + 1)).astype(jnp.float32).reshape(-1)

    def team_update(team_items):
        section_team, start_team, wave_index = team_items
        forcing = test_field(wave_index, TESTS, LEV)
        spec_field = section_team.astype(jnp.float32) + forcing[:, :, :, None, None] * part_pick[:, None] * anchor_rows[None, :]
        spec_field = spec_field.astype(jnp.bfloat16).reshape(TESTS, 3, LEV, 2, pair_count, NM + 1)
        masked = (spec_field[:, :, :, :, :, None, :] * masks_low).astype(jnp.float32)
        spectra = jnp.einsum('scvpqhr,rqa->ascvpqh', masked, legendre)
        spectra = spectra.astype(jnp.bfloat16).astype(jnp.float32).reshape(NLAT, TESTS, 3, LEV, 2, NM)
        grid_field = jnp.einsum('ascvpm,pmo->ascvo', spectra, inverse_table)
        emf = cross_field(velocity[:, None], grid_field, 2).astype(jnp.bfloat16).astype(jnp.float32)
        fourier = jnp.einsum('ascvo,pmo->ascvpm', emf, forward_table)
        fourier = (fourier * weights[:, None, None, None, None, None]).astype(jnp.bfloat16).astype(jnp.float32)
        fourier = fourier.reshape(NLAT, TESTS, 3, LEV, 2, pair_count, 2)
        project = jnp.einsum('ascvpqh,rqa->scvpqhr', fourier, legendre)
        tendency = lax.optimization_barrier(jnp.sum(project * masks_real, axis=5)).reshape(TESTS, 3, LEV, 2, -1)
        return start_team + step_weight * (tendency - diffusion * spread * section_team.astype(jnp.float32))
    return lax.map(team_update, (section, start, wavenumber))
```

```python
import math

import jax
import jax.numpy as jnp
from jax import lax
from jax.experimental import pallas as pl
from jax.experimental.pallas import tpu as pltpu
from jax.sharding import Mesh, PartitionSpec as P

NM = 256
NLAT = 384
NLON = 768
LEV = 24
TESTS = 2


grid_scale = 1.0 / 64.0
anchor_gain = 64.0 * math.sqrt(4.0 * math.pi)
quadrature_gain = 64.0
diffusion = 7e-06
step_weight = 2.0
row_block = 16


def seed_values(order_real, order_count, sine_theta):
    factor_index = jnp.arange(1, order_count, dtype=jnp.float32)
    factor_log = jnp.log((2.0 * factor_index - 1.0) / (2.0 * factor_index))
    partial_log = jnp.sum(
        jnp.where(factor_index[None, :] <= order_real[:, None], factor_log[None, :], 0.0), axis=1
    )
    seed_log = 0.5 * (jnp.log((2.0 * order_real + 1.0) / (4.0 * jnp.pi)) + partial_log)
    return jnp.exp(seed_log[:, None] + order_real[:, None] * jnp.log(sine_theta)[None, :])


def pair_table(pair_ids, order_count, lat_count):
    pair_count = pair_ids.shape[0]
    order_low = pair_ids.astype(jnp.float32)
    order_high = (order_count - 1 - pair_ids).astype(jnp.float32)
    colatitude = jnp.pi * (jnp.arange(lat_count, dtype=jnp.float32) + 0.5) / lat_count
    cosine = jnp.cos(colatitude)
    sine_theta = jnp.sin(colatitude)
    seed_low = seed_values(order_low, order_count, sine_theta)
    seed_high = seed_values(order_high, order_count, sine_theta)
    switch_row = order_count - pair_ids

    def one_row(state_pair, row_id):
        latest, before = state_pair
        in_low = row_id < switch_row
        degree = jnp.where(in_low, pair_ids + row_id, row_id - 1)
        order_real = jnp.where(in_low, order_low, order_high)
        degree_real = degree.astype(jnp.float32)
        active = degree_real > order_real
        divisor = jnp.where(active, degree_real * degree_real - order_real * order_real, 1.0)
        upper = jnp.sqrt(jnp.maximum(4.0 * degree_real * degree_real - 1.0, 0.0) / divisor)
        lower_num = ((degree_real - 1.0) * (degree_real - 1.0) - order_real * order_real) * (
            2.0 * degree_real + 1.0
        )
        lower = jnp.sqrt(
            jnp.maximum(lower_num, 0.0) / (divisor * jnp.maximum(2.0 * degree_real - 3.0, 1.0))
        )
        recurred = upper[:, None] * cosine[None, :] * latest - lower[:, None] * before
        is_seed = (row_id == 0) | (row_id == switch_row)
        seeded = jnp.where(in_low[:, None], seed_low, seed_high)
        current = jnp.where(is_seed[:, None], seeded, jnp.where(active[:, None], recurred, 0.0))
        return ((current, latest), current)

    def block_rows(state_pair, first_row):
        produced = []
        for offset in range(row_block):
            state_pair, current = one_row(state_pair, first_row + offset)
            produced.append(current)
        return (state_pair, jnp.stack(produced))

    turns = -(-(order_count + 1) // row_block)
    blank_rows = jnp.zeros((pair_count, lat_count), jnp.float32)
    firsts = jnp.arange(turns, dtype=jnp.int32) * row_block
    _, values = lax.scan(block_rows, (blank_rows, blank_rows), firsts)
    leg_table = values.reshape(turns * row_block, pair_count, lat_count)[: order_count + 1]
    row_index = jnp.arange(order_count + 1, dtype=jnp.int32)
    first_half = row_index[None, :] < (order_count - pair_ids)[:, None]
    degree = jnp.where(first_half, pair_ids[:, None] + row_index[None, :], row_index[None, :] - 1)
    return (leg_table, first_half, degree)


def wave_table(order_list, lon_count):
    longitude = jnp.arange(lon_count, dtype=jnp.int32)
    phase_index = order_list[:, None] * longitude[None, :] % lon_count
    angle_rad = 2.0 * jnp.pi / lon_count * phase_index.astype(jnp.float32)
    return jnp.stack([jnp.cos(angle_rad), jnp.sin(angle_rad)])


def lat_weights(latitudes, lat_count):
    colatitude = jnp.pi * (latitudes.astype(jnp.float32) + 0.5) / lat_count
    return quadrature_gain * (jnp.pi / lat_count) * jnp.sin(colatitude)


def test_field(wave_index, test_count, levels):
    component = jnp.arange(3, dtype=jnp.int32)
    test_ids = jnp.arange(test_count, dtype=jnp.int32)
    level_ids = jnp.arange(levels, dtype=jnp.float32)
    aligned = (component[None, :] == test_ids[:, None]).astype(jnp.float32)
    profile = jnp.cos(jnp.pi * wave_index.astype(jnp.float32) * (level_ids + 0.5) / levels)
    return anchor_gain * aligned[:, :, None] * profile[None, None, :]


def cross_field(motion, magnetic, along):
    return jnp.roll(motion, -1, along) * jnp.roll(magnetic, -2, along) - jnp.roll(
        motion, -2, along
    ) * jnp.roll(magnetic, -1, along)


def shards_general(section, start, velocity, pair_list, wavenumber):
    pair_count = pair_list.shape[0]
    leg_table, first_half, degree = pair_table(pair_list, NM, NLAT)
    legendre = leg_table.astype(jnp.bfloat16)
    selectors = jnp.stack([first_half, jnp.logical_not(first_half)], axis=1)
    masks_low = selectors.astype(jnp.bfloat16)
    anchor = (pair_list == 0)[:, None] & (jnp.arange(NM + 1) == 0)[None, :]
    anchor_rows = anchor.reshape(-1).astype(jnp.float32)
    part_pick = jnp.array([1.0, 0.0], jnp.float32)
    forcing = test_field(wavenumber[0], TESTS, LEV)
    spec_field = (
        section[0].astype(jnp.float32)
        + forcing[:, :, :, None, None] * part_pick[:, None] * anchor_rows[None, :]
    )
    spec_field = spec_field.astype(jnp.bfloat16).reshape(TESTS, 3, LEV, 2, pair_count, NM + 1)
    masked = spec_field[:, :, :, :, :, None, :] * masks_low
    spectra = jnp.einsum(
        "scvpqhr,rqa->ascvpqh", masked, legendre, preferred_element_type=jnp.float32
    )
    spectra = spectra.astype(jnp.bfloat16).reshape(NLAT, TESTS, 3, LEV, 2, 2 * pair_count)
    every_pair = lax.all_gather(pair_list, "ma", axis=0, tiled=True)
    order_list = jnp.stack([every_pair, NM - 1 - every_pair], axis=1).reshape(-1)
    waves = wave_table(order_list, NLON)
    inverse_table = (waves * grid_scale).astype(jnp.bfloat16)
    forward_table = (waves * (2.0 * jnp.pi / NLON)).astype(jnp.bfloat16)
    wind_field = lax.all_gather(velocity, "team", axis=2, tiled=True)
    band_size = velocity.shape[0]
    latitudes = lax.axis_index("ma") * band_size + jnp.arange(band_size, dtype=jnp.int32)
    weights = lat_weights(latitudes, NLAT)
    collected = []
    for test_id in range(TESTS):
        grid_field = jnp.einsum(
            "ascvpm,pmo->ascvo",
            lax.all_to_all(
                spectra[:, test_id : test_id + 1], "ma", split_axis=0, concat_axis=5, tiled=True
            ),
            inverse_table,
            preferred_element_type=jnp.float32,
        )
        emf = cross_field(wind_field[:, None], grid_field, 2).astype(jnp.bfloat16)
        fourier = jnp.einsum(
            "ascvo,pmo->ascvpm", emf, forward_table, preferred_element_type=jnp.float32
        )
        fourier = (fourier * weights[:, None, None, None, None, None]).astype(jnp.bfloat16)
        collected.append(lax.all_to_all(fourier, "ma", split_axis=5, concat_axis=0, tiled=True))
    returned = jnp.concatenate(collected, axis=1)
    returned = returned.reshape(NLAT, TESTS, 3, LEV, 2, pair_count, 2)
    project = jnp.einsum(
        "ascvpqh,rqa->scvpqhr", returned, legendre, preferred_element_type=jnp.float32
    )
    tendency = jnp.sum(project * selectors.astype(jnp.float32), axis=5).reshape(
        TESTS, 3, LEV, 2, -1
    )
    spread = (degree * (degree + 1)).astype(jnp.float32).reshape(-1)
    updated = start[0] + step_weight * (
        tendency - diffusion * spread * section[0].astype(jnp.float32)
    )
    return updated[None]


BF16 = jnp.bfloat16
F32 = jnp.float32
VMEM_CAP = 56 << 20
PAIR_ROWS = NM + 1
CHUNK_ROWS = 16
SLOTS = 8


def table_window(slots):
    return -(-(PAIR_ROWS + slots - 1) // 32) * 32


def swap_major(block):
    return jnp.swapaxes(block, 0, 1)


def table_kernel(upper, lower, first, second, seed_low, seed_high, cosine, out):
    shape = seed_low.shape
    cosine_rows = jnp.broadcast_to(cosine[...], shape)
    first_step = first[...]
    second_step = second[...]
    low_value = seed_low[...]
    high_value = seed_high[...]

    def chunk(index, state):
        latest, before = state
        scale_up = upper[index]
        scale_down = lower[index]
        produced = []
        for offset in range(CHUNK_ROWS):
            step = index * CHUNK_ROWS + offset
            recurred = (scale_up[:, offset : offset + 1] * cosine_rows) * latest - scale_down[
                :, offset : offset + 1
            ] * before
            current = jnp.where(
                first_step == step,
                low_value,
                jnp.where(second_step == step, high_value, recurred),
            )
            produced.append(current)
            latest, before = current, latest
        rows = swap_major(jnp.stack(produced))
        out[:, pl.ds(pl.multiple_of(index * CHUNK_ROWS, CHUNK_ROWS), CHUNK_ROWS), :] = rows.astype(
            BF16
        )
        return latest, before

    blank = jnp.zeros(shape, F32)
    lax.fori_loop(0, out.shape[1] // CHUNK_ROWS, chunk, (blank, blank))


def legendre_table(every_pair, slots, lats):
    pairs = every_pair.shape[0]
    window = table_window(slots)
    order_low = every_pair.astype(F32)
    order_high = (NM - 1 - every_pair).astype(F32)
    colatitude = jnp.pi * (lats.astype(F32) + 0.5) / NLAT
    seed_low = seed_values(order_low, NM, jnp.sin(colatitude))
    seed_high = seed_values(order_high, NM, jnp.sin(colatitude))
    slot = jnp.arange(pairs, dtype=jnp.int32) % slots
    row = jnp.arange(window, dtype=jnp.int32)[None, :] - slot[:, None]
    switch = NM - every_pair
    in_low = row < switch[:, None]
    degree = jnp.where(in_low, every_pair[:, None] + row, row - 1)
    order = jnp.where(in_low, order_low[:, None], order_high[:, None])
    real = degree.astype(F32)
    active = (real > order) & (row >= 0) & (row < PAIR_ROWS)
    divisor = jnp.where(active, real * real - order * order, 1.0)
    upper = jnp.sqrt(jnp.maximum(4.0 * real * real - 1.0, 0.0) / divisor)
    lower_num = ((real - 1.0) * (real - 1.0) - order * order) * (2.0 * real + 1.0)
    lower = jnp.sqrt(
        jnp.maximum(lower_num, 0.0) / (divisor * jnp.maximum(2.0 * real - 3.0, 1.0))
    )
    by_chunk = lambda values: jnp.swapaxes(
        jnp.where(active, values, 0.0).reshape(pairs, window // CHUNK_ROWS, CHUNK_ROWS), 0, 1
    )
    spread_out = lambda values: jnp.broadcast_to(values[:, None], (pairs, NLAT))
    chunks = window // CHUNK_ROWS
    coefficient = pl.BlockSpec((chunks, 8, CHUNK_ROWS), lambda q: (0, q, 0))
    per_pair = pl.BlockSpec((8, NLAT), lambda q: (q, 0))
    return pl.pallas_call(
        table_kernel,
        grid=(pairs // 8,),
        in_specs=[coefficient, coefficient, per_pair, per_pair, per_pair, per_pair]
        + [pl.BlockSpec((1, NLAT), lambda q: (0, 0))],
        out_specs=pl.BlockSpec((8, window, NLAT), lambda q: (q, 0, 0)),
        out_shape=jax.ShapeDtypeStruct((pairs, window, NLAT), BF16),
        compiler_params=pltpu.CompilerParams(vmem_limit_bytes=VMEM_CAP),
        name="table",
    )(
        by_chunk(upper),
        by_chunk(lower),
        spread_out(slot),
        spread_out(slot + switch),
        seed_low,
        seed_high,
        jnp.cos(colatitude)[None, :],
    )


def synthesis_kernel(switch, spec, table, out):
    source, group = pl.program_id(0), pl.program_id(1)
    groups = pl.num_programs(1)
    window = table.shape[1]
    fields = spec.shape[1]
    lane = lax.broadcasted_iota(jnp.int32, (fields, window), 1)
    collected = []
    for slot in range(SLOTS):
        start = pl.multiple_of((group * SLOTS + slot) * NM, NM)
        rows = spec[0, :, pl.ds(start, window)].astype(F32)
        in_low = lane < switch[(source * groups + group) * SLOTS + slot]
        both = jnp.concatenate([jnp.where(in_low, rows, 0.0), jnp.where(in_low, 0.0, rows)], axis=0)
        made = jnp.dot(both.astype(BF16), table[slot], preferred_element_type=F32)
        collected += [made[:fields], made[fields:]]
    out[...] = swap_major(jnp.stack(collected)).astype(BF16)


def synthesis(spec, table, switch, slots):
    sources, fields, width = spec.shape
    pairs, window, _ = table.shape
    groups = slots // SLOTS
    return pl.pallas_call(
        synthesis_kernel,
        grid_spec=pltpu.PrefetchScalarGridSpec(
            num_scalar_prefetch=1,
            grid=(sources, groups),
            in_specs=[
                pl.BlockSpec((1, fields, width), lambda z, g, _: (z, 0, 0)),
                pl.BlockSpec((SLOTS, window, NLAT), lambda z, g, _: (z * groups + g, 0, 0)),
            ],
            out_specs=pl.BlockSpec(
                (fields, 2 * SLOTS, NLAT), lambda z, g, _: (0, z * groups + g, 0)
            ),
        ),
        out_shape=jax.ShapeDtypeStruct((fields, 2 * pairs, NLAT), BF16),
        compiler_params=pltpu.CompilerParams(vmem_limit_bytes=VMEM_CAP),
        name="synthesis",
    )(switch, spec, table)


LON_TILE = 256


def grid_kernel(spectra, wind, inverse_cos, inverse_sin, forward_cos, forward_sin, weights, out, emf):
    for tile in range(NLON // LON_TILE):
        span = pl.ds(tile * LON_TILE, LON_TILE)
        magnetic = [
            jnp.dot(inverse_cos[span, :], spectra[2 * c], preferred_element_type=F32)
            + jnp.dot(inverse_sin[span, :], spectra[2 * c + 1], preferred_element_type=F32)
            for c in range(3)
        ]
        motion = [wind[c, span, :].astype(F32) for c in range(3)]
        for c in range(3):
            one, two = (c + 1) % 3, (c + 2) % 3
            emf[c, span, :] = (
                motion[one] * magnetic[two] - motion[two] * magnetic[one]
            ).astype(BF16)
    scale = weights[...]
    for c in range(3):
        for part, table in enumerate((forward_cos, forward_sin)):
            back = jnp.dot(table[...], emf[c], preferred_element_type=F32)
            out[2 * c + part] = (back * scale).astype(BF16)


def grid_product(spectra, wind, tables, weights):
    fields, orders, lats = spectra.shape
    whole = lambda array: pl.BlockSpec(array.shape, lambda g: (0,) * array.ndim)
    per_group = pl.BlockSpec((6, orders, lats), lambda g: (g, 0, 0))
    return pl.pallas_call(
        grid_kernel,
        grid=(fields // 6,),
        in_specs=[per_group, whole(wind)] + [whole(table) for table in tables] + [whole(weights)],
        out_specs=per_group,
        out_shape=jax.ShapeDtypeStruct(spectra.shape, BF16),
        scratch_shapes=[pltpu.VMEM((3, NLON, lats), BF16)],
        compiler_params=pltpu.CompilerParams(vmem_limit_bytes=VMEM_CAP),
        name="grid_product",
    )(spectra, wind, *tables, weights)


def analysis_kernel(switch, fourier, table, out, carry):
    source, group = pl.program_id(0), pl.program_id(1)
    groups = pl.num_programs(1)
    window = table.shape[1]
    fields = fourier.shape[0]
    lane = lax.broadcasted_iota(jnp.int32, (fields, window), 1)
    by_order = swap_major(fourier[...].astype(F32)).astype(BF16)

    @pl.when(group == 0)
    def _():
        carry[...] = jnp.zeros_like(carry)

    over = carry[...]
    blank = jnp.zeros((fields, 128 - (window - NM)), F32)
    for slot in range(SLOTS):
        both = jnp.concatenate([by_order[2 * slot], by_order[2 * slot + 1]], axis=0)
        made = lax.dot_general(
            both, table[slot], (((1,), (1,)), ((), ())), preferred_element_type=F32
        )
        in_low = lane < switch[(source * groups + group) * SLOTS + slot]
        rows = jnp.where(in_low, made[:fields], made[fields:])
        start = pl.multiple_of((group * SLOTS + slot) * NM, NM)
        out[0, :, pl.ds(start, 128)] = (rows[:, :128] + over).astype(BF16)
        out[0, :, pl.ds(start + 128, NM - 128)] = rows[:, 128:NM].astype(BF16)
        over = jnp.concatenate([rows[:, NM:], blank], axis=1)
    carry[...] = over

    @pl.when(group == groups - 1)
    def _():
        width = out.shape[2]
        full = width // NM * NM
        out[0, :, full:] = over[:, : width - full].astype(BF16)


def analysis(fourier, table, switch, slots, width):
    fields, orders, lats = fourier.shape
    pairs, window, _ = table.shape
    groups = slots // SLOTS
    return pl.pallas_call(
        analysis_kernel,
        grid_spec=pltpu.PrefetchScalarGridSpec(
            num_scalar_prefetch=1,
            grid=(pairs // slots, groups),
            in_specs=[
                pl.BlockSpec((fields, 2 * SLOTS, NLAT), lambda z, g, _: (0, z * groups + g, 0)),
                pl.BlockSpec((SLOTS, window, NLAT), lambda z, g, _: (z * groups + g, 0, 0)),
            ],
            out_specs=pl.BlockSpec((1, fields, width), lambda z, g, _: (z, 0, 0)),
            scratch_shapes=[pltpu.VMEM((fields, 128), F32)],
        ),
        out_shape=jax.ShapeDtypeStruct((pairs // slots, fields, width), BF16),
        compiler_params=pltpu.CompilerParams(vmem_limit_bytes=VMEM_CAP),
        name="analysis",
    )(switch, fourier, table)


def gather_pairs(pair_list, count):
    own = pair_list.shape[0]
    place = lax.axis_index("ma")
    every = jnp.zeros((count, own), jnp.int32)
    every = lax.dynamic_update_slice(every, pair_list[None], (place, 0))
    for shift in range(1, count):
        moved = lax.ppermute(pair_list, "ma", [(k, (k + shift) % count) for k in range(count)])
        every = lax.dynamic_update_slice(every, moved[None], ((place - shift) % count, 0))
    return every.reshape(-1)


def shards_by_level(section, start, velocity, pair_list, wavenumber, *, count):
    slots = pair_list.shape[0]
    width = section.shape[-1]
    depth = LEV // (2 * count)
    band = velocity.shape[0]
    half = band // 2
    every_pair = gather_pairs(pair_list, count)
    slot_of = jnp.arange(count * slots, dtype=jnp.int32) % slots
    switch = slot_of + NM - every_pair

    anchor = (pair_list == 0)[:, None] & (jnp.arange(PAIR_ROWS) == 0)[None, :]
    anchor_rows = anchor.reshape(-1).astype(F32)
    part_pick = jnp.array([1.0, 0.0], F32)
    forcing = test_field(wavenumber[0], TESTS, LEV)
    spec_field = (
        section[0].astype(F32)
        + forcing[:, :, :, None, None] * part_pick[:, None] * anchor_rows[None, :]
    ).astype(BF16)
    spec_field = spec_field.reshape(TESTS * 3, 2 * count, depth, 2, width)

    split = velocity.reshape(2, half, 3, LEV // 4, NLON)
    split = lax.all_to_all(split, "k", split_axis=0, concat_axis=0, tiled=True)
    split = split.transpose(0, 3, 1, 2, 4).reshape(count, depth, half, 3, NLON)

    lats = jnp.arange(NLAT, dtype=jnp.int32).reshape(count, 2, half).swapaxes(0, 1).reshape(-1)
    table = legendre_table(every_pair, slots, lats)
    order_list = jnp.stack([every_pair, NM - 1 - every_pair], axis=1).reshape(-1)
    waves = wave_table(order_list, NLON)
    inverse_table = (waves * grid_scale).astype(BF16)
    forward_table = (waves * (2.0 * jnp.pi / NLON)).astype(BF16)
    tables = (inverse_table[0].T, inverse_table[1].T, forward_table[0], forward_table[1])
    weights = lat_weights(lats, NLAT)[None, :]

    across = lax.axis_index("x")
    core = lax.axis_index("k")
    own_first = (across == 0) & (core == 0)
    own_second = (across == 1) & (core == 1)
    returned = []
    for level in range(depth):
        sent = spec_field[:, :, level].swapaxes(0, 1)
        arrived = lax.all_to_all(sent, ("k", "ma"), split_axis=0, concat_axis=0, tiled=True)
        spec = arrived.reshape(2, count, TESTS * 6, width).swapaxes(0, 1)
        spec = spec.reshape(count, TESTS * 12, width)
        spectra = synthesis(spec, table, switch, slots)

        held = lax.all_to_all(split[:, level], "ma", split_axis=0, concat_axis=0, tiled=True)
        turn = lax.ppermute(held, ("x", "k"), [(0, 2), (1, 0), (2, 3), (3, 1)])
        cross = lax.ppermute(held, ("x", "k"), [(1, 2), (2, 1)])
        first = jnp.where(own_first, held, jnp.where((across == 0) & (core == 1), cross, turn))
        second = jnp.where(own_second, held, jnp.where((across == 1) & (core == 0), cross, turn))
        wind = jnp.stack([first, second]).reshape(NLAT, 3, NLON).transpose(1, 2, 0)

        fourier = grid_product(spectra, wind, tables, weights)
        tendency = analysis(fourier, table, switch, slots, width)
        back = tendency.reshape(count, 2, TESTS * 3, 2, width).swapaxes(0, 1)
        back = back.reshape(2 * count, TESTS * 3, 2, width)
        returned.append(
            lax.all_to_all(back, ("k", "ma"), split_axis=0, concat_axis=0, tiled=True)
        )
    tendency = jnp.stack(returned, axis=1).reshape(LEV, TESTS, 3, 2, width)
    tendency = tendency.transpose(1, 2, 0, 3, 4).astype(F32)

    row_index = jnp.arange(PAIR_ROWS, dtype=jnp.int32)
    first_half = row_index[None, :] < (NM - pair_list)[:, None]
    degree = jnp.where(first_half, pair_list[:, None] + row_index[None, :], row_index[None, :] - 1)
    spread = (degree * (degree + 1)).astype(F32).reshape(-1)
    updated = start[0] + step_weight * (tendency - diffusion * spread * section[0].astype(F32))
    return updated[None]


def solution(mesh):
    sizes = dict(mesh.shape)
    count = sizes["ma"]
    whole_slots = (NM // 2) % (count * SLOTS) == 0
    if sizes["team"] == 4 and LEV % (2 * count) == 0 and whole_slots:
        grid = Mesh(
            mesh.devices.reshape(sizes["run"], 2, 2, count), ("run", "x", "k", "ma")
        )
        team = ("x", "k")
        body = lambda *arrays: shards_by_level(*arrays, count=count)
    else:
        grid, team, body = mesh, ("team",), shards_general
    placed = (
        P(("run",) + team, None, None, None, None, "ma"),
        P(("run",) + team, None, None, None, None, "ma"),
        P(("run", "ma"), None, team, None),
        P("ma"),
        P(team),
    )
    return jax.shard_map(
        body,
        mesh=grid,
        in_specs=placed,
        out_specs=P(("run",) + team, None, None, None, None, "ma"),
        check_vma=False,
    )
```

```python
import functools
import math

import jax
import jax.numpy as jnp
from jax import lax
from jax.experimental import pallas as pl
from jax.experimental.pallas import tpu as pltpu
from jax.sharding import Mesh, PartitionSpec as P

NM = 256
NLAT = 384
NLON = 768
LEV = 24
TESTS = 2


grid_scale = 1.0 / 64.0
anchor_gain = 64.0 * math.sqrt(4.0 * math.pi)
quadrature_gain = 64.0
diffusion = 7e-06
step_weight = 2.0
row_block = 16


def seed_values(order_real, order_count, sine_theta):
    factor_index = jnp.arange(1, order_count, dtype=jnp.float32)
    factor_log = jnp.log((2.0 * factor_index - 1.0) / (2.0 * factor_index))
    partial_log = jnp.sum(
        jnp.where(factor_index[None, :] <= order_real[:, None], factor_log[None, :], 0.0), axis=1
    )
    seed_log = 0.5 * (jnp.log((2.0 * order_real + 1.0) / (4.0 * jnp.pi)) + partial_log)
    return jnp.exp(seed_log[:, None] + order_real[:, None] * jnp.log(sine_theta)[None, :])


def pair_table(pair_ids, order_count, lat_count):
    pair_count = pair_ids.shape[0]
    order_low = pair_ids.astype(jnp.float32)
    order_high = (order_count - 1 - pair_ids).astype(jnp.float32)
    colatitude = jnp.pi * (jnp.arange(lat_count, dtype=jnp.float32) + 0.5) / lat_count
    cosine = jnp.cos(colatitude)
    sine_theta = jnp.sin(colatitude)
    seed_low = seed_values(order_low, order_count, sine_theta)
    seed_high = seed_values(order_high, order_count, sine_theta)
    switch_row = order_count - pair_ids

    def one_row(state_pair, row_id):
        latest, before = state_pair
        in_low = row_id < switch_row
        degree = jnp.where(in_low, pair_ids + row_id, row_id - 1)
        order_real = jnp.where(in_low, order_low, order_high)
        degree_real = degree.astype(jnp.float32)
        active = degree_real > order_real
        divisor = jnp.where(active, degree_real * degree_real - order_real * order_real, 1.0)
        upper = jnp.sqrt(jnp.maximum(4.0 * degree_real * degree_real - 1.0, 0.0) / divisor)
        lower_num = ((degree_real - 1.0) * (degree_real - 1.0) - order_real * order_real) * (
            2.0 * degree_real + 1.0
        )
        lower = jnp.sqrt(
            jnp.maximum(lower_num, 0.0) / (divisor * jnp.maximum(2.0 * degree_real - 3.0, 1.0))
        )
        recurred = upper[:, None] * cosine[None, :] * latest - lower[:, None] * before
        is_seed = (row_id == 0) | (row_id == switch_row)
        seeded = jnp.where(in_low[:, None], seed_low, seed_high)
        current = jnp.where(is_seed[:, None], seeded, jnp.where(active[:, None], recurred, 0.0))
        return ((current, latest), current)

    def block_rows(state_pair, first_row):
        produced = []
        for offset in range(row_block):
            state_pair, current = one_row(state_pair, first_row + offset)
            produced.append(current)
        return (state_pair, jnp.stack(produced))

    turns = -(-(order_count + 1) // row_block)
    blank_rows = jnp.zeros((pair_count, lat_count), jnp.float32)
    firsts = jnp.arange(turns, dtype=jnp.int32) * row_block
    _, values = lax.scan(block_rows, (blank_rows, blank_rows), firsts)
    leg_table = values.reshape(turns * row_block, pair_count, lat_count)[: order_count + 1]
    row_index = jnp.arange(order_count + 1, dtype=jnp.int32)
    first_half = row_index[None, :] < (order_count - pair_ids)[:, None]
    degree = jnp.where(first_half, pair_ids[:, None] + row_index[None, :], row_index[None, :] - 1)
    return (leg_table, first_half, degree)


def wave_table(order_list, lon_count):
    longitude = jnp.arange(lon_count, dtype=jnp.int32)
    phase_index = order_list[:, None] * longitude[None, :] % lon_count
    angle_rad = 2.0 * jnp.pi / lon_count * phase_index.astype(jnp.float32)
    return jnp.stack([jnp.cos(angle_rad), jnp.sin(angle_rad)])


def lat_weights(latitudes, lat_count):
    colatitude = jnp.pi * (latitudes.astype(jnp.float32) + 0.5) / lat_count
    return quadrature_gain * (jnp.pi / lat_count) * jnp.sin(colatitude)


def test_field(wave_index, test_count, levels):
    component = jnp.arange(3, dtype=jnp.int32)
    test_ids = jnp.arange(test_count, dtype=jnp.int32)
    level_ids = jnp.arange(levels, dtype=jnp.float32)
    aligned = (component[None, :] == test_ids[:, None]).astype(jnp.float32)
    profile = jnp.cos(jnp.pi * wave_index.astype(jnp.float32) * (level_ids + 0.5) / levels)
    return anchor_gain * aligned[:, :, None] * profile[None, None, :]


def cross_field(motion, magnetic, along):
    return jnp.roll(motion, -1, along) * jnp.roll(magnetic, -2, along) - jnp.roll(
        motion, -2, along
    ) * jnp.roll(magnetic, -1, along)


def shards_general(section, start, velocity, pair_list, wavenumber):
    pair_count = pair_list.shape[0]
    leg_table, first_half, degree = pair_table(pair_list, NM, NLAT)
    legendre = leg_table.astype(jnp.bfloat16)
    selectors = jnp.stack([first_half, jnp.logical_not(first_half)], axis=1)
    masks_low = selectors.astype(jnp.bfloat16)
    anchor = (pair_list == 0)[:, None] & (jnp.arange(NM + 1) == 0)[None, :]
    anchor_rows = anchor.reshape(-1).astype(jnp.float32)
    part_pick = jnp.array([1.0, 0.0], jnp.float32)
    forcing = test_field(wavenumber[0], TESTS, LEV)
    spec_field = (
        section[0].astype(jnp.float32)
        + forcing[:, :, :, None, None] * part_pick[:, None] * anchor_rows[None, :]
    )
    spec_field = spec_field.astype(jnp.bfloat16).reshape(TESTS, 3, LEV, 2, pair_count, NM + 1)
    masked = spec_field[:, :, :, :, :, None, :] * masks_low
    spectra = jnp.einsum(
        "scvpqhr,rqa->ascvpqh", masked, legendre, preferred_element_type=jnp.float32
    )
    spectra = spectra.astype(jnp.bfloat16).reshape(NLAT, TESTS, 3, LEV, 2, 2 * pair_count)
    every_pair = lax.all_gather(pair_list, "ma", axis=0, tiled=True)
    order_list = jnp.stack([every_pair, NM - 1 - every_pair], axis=1).reshape(-1)
    waves = wave_table(order_list, NLON)
    inverse_table = (waves * grid_scale).astype(jnp.bfloat16)
    forward_table = (waves * (2.0 * jnp.pi / NLON)).astype(jnp.bfloat16)
    wind_field = lax.all_gather(velocity, "team", axis=2, tiled=True)
    band_size = velocity.shape[0]
    latitudes = lax.axis_index("ma") * band_size + jnp.arange(band_size, dtype=jnp.int32)
    weights = lat_weights(latitudes, NLAT)
    collected = []
    for test_id in range(TESTS):
        grid_field = jnp.einsum(
            "ascvpm,pmo->ascvo",
            lax.all_to_all(
                spectra[:, test_id : test_id + 1], "ma", split_axis=0, concat_axis=5, tiled=True
            ),
            inverse_table,
            preferred_element_type=jnp.float32,
        )
        emf = cross_field(wind_field[:, None], grid_field, 2).astype(jnp.bfloat16)
        fourier = jnp.einsum(
            "ascvo,pmo->ascvpm", emf, forward_table, preferred_element_type=jnp.float32
        )
        fourier = (fourier * weights[:, None, None, None, None, None]).astype(jnp.bfloat16)
        collected.append(lax.all_to_all(fourier, "ma", split_axis=5, concat_axis=0, tiled=True))
    returned = jnp.concatenate(collected, axis=1)
    returned = returned.reshape(NLAT, TESTS, 3, LEV, 2, pair_count, 2)
    project = jnp.einsum(
        "ascvpqh,rqa->scvpqhr", returned, legendre, preferred_element_type=jnp.float32
    )
    tendency = jnp.sum(project * selectors.astype(jnp.float32), axis=5).reshape(
        TESTS, 3, LEV, 2, -1
    )
    spread = (degree * (degree + 1)).astype(jnp.float32).reshape(-1)
    updated = start[0] + step_weight * (
        tendency - diffusion * spread * section[0].astype(jnp.float32)
    )
    return updated[None]


BF16 = jnp.bfloat16
F32 = jnp.float32
VMEM_CAP = 56 << 20
PAIR_ROWS = NM + 1
CHUNK_ROWS = 16
SLOTS = 8


def work(micros):
    return pl.CostEstimate(
        flops=int(micros * 1e9), transcendentals=0, bytes_accessed=int(micros * 1e6)
    )


def after(value, *others):
    return lax.optimization_barrier((value,) + others)[0]


def table_window(slots):
    return -(-(PAIR_ROWS + slots - 1) // 32) * 32


def swap_major(block):
    return jnp.swapaxes(block, 0, 1)


def table_kernel(upper, lower, first, second, seed_low, seed_high, cosine, out, *, lead):
    shape = seed_low.shape
    cosine_rows = jnp.broadcast_to(cosine[...], shape)
    first_step = first[...]
    second_step = second[...]
    low_value = seed_low[...]
    high_value = seed_high[...]

    def chunk(starting, index, state):
        latest, before = state
        scale_up = upper[index]
        scale_down = lower[index]
        produced = []
        for offset in range(CHUNK_ROWS):
            step = index * CHUNK_ROWS + offset
            current = (scale_up[:, offset : offset + 1] * cosine_rows) * latest - scale_down[
                :, offset : offset + 1
            ] * before
            current = jnp.where(second_step == step, high_value, current)
            if starting:
                current = jnp.where(first_step == step, low_value, current)
            produced.append(current)
            latest, before = current, latest
        rows = swap_major(jnp.stack(produced))
        out[:, pl.ds(pl.multiple_of(index * CHUNK_ROWS, CHUNK_ROWS), CHUNK_ROWS), :] = rows.astype(
            BF16
        )
        return latest, before

    blank = jnp.zeros(shape, F32)
    state = lax.fori_loop(0, lead, functools.partial(chunk, True), (blank, blank))
    lax.fori_loop(lead, out.shape[1] // CHUNK_ROWS, functools.partial(chunk, False), state)


def legendre_table(every_pair, slots, lats):
    pairs = every_pair.shape[0]
    window = table_window(slots)
    order_low = every_pair.astype(F32)
    order_high = (NM - 1 - every_pair).astype(F32)
    colatitude = jnp.pi * (lats.astype(F32) + 0.5) / NLAT
    seed_low = seed_values(order_low, NM, jnp.sin(colatitude))
    seed_high = seed_values(order_high, NM, jnp.sin(colatitude))
    slot = jnp.arange(pairs, dtype=jnp.int32) % slots
    row = jnp.arange(window, dtype=jnp.int32)[None, :] - slot[:, None]
    switch = NM - every_pair
    in_low = row < switch[:, None]
    degree = jnp.where(in_low, every_pair[:, None] + row, row - 1)
    order = jnp.where(in_low, order_low[:, None], order_high[:, None])
    real = degree.astype(F32)
    active = (real > order) & (row >= 0) & (row < PAIR_ROWS)
    divisor = jnp.where(active, real * real - order * order, 1.0)
    upper = jnp.sqrt(jnp.maximum(4.0 * real * real - 1.0, 0.0) / divisor)
    lower_num = ((real - 1.0) * (real - 1.0) - order * order) * (2.0 * real + 1.0)
    lower = jnp.sqrt(
        jnp.maximum(lower_num, 0.0) / (divisor * jnp.maximum(2.0 * real - 3.0, 1.0))
    )
    by_chunk = lambda values: jnp.swapaxes(
        jnp.where(active, values, 0.0).reshape(pairs, window // CHUNK_ROWS, CHUNK_ROWS), 0, 1
    )
    lanes = lats.shape[0]
    spread_out = lambda values: jnp.broadcast_to(values[:, None], (pairs, lanes))
    chunks = window // CHUNK_ROWS
    coefficient = pl.BlockSpec((chunks, 8, CHUNK_ROWS), lambda q: (0, q, 0))
    per_pair = pl.BlockSpec((8, lanes), lambda q: (q, 0))
    lead = -(-slots // CHUNK_ROWS)
    return pl.pallas_call(
        functools.partial(table_kernel, lead=lead),
        grid=(pairs // 8,),
        in_specs=[coefficient, coefficient, per_pair, per_pair, per_pair, per_pair]
        + [pl.BlockSpec((1, lanes), lambda q: (0, 0))],
        out_specs=pl.BlockSpec((8, window, lanes), lambda q: (q, 0, 0)),
        out_shape=jax.ShapeDtypeStruct((pairs, window, lanes), BF16),
        compiler_params=pltpu.CompilerParams(vmem_limit_bytes=VMEM_CAP),
        cost_estimate=work(40),
        name="table",
    )(
        by_chunk(upper),
        by_chunk(lower),
        spread_out(slot),
        spread_out(slot + switch),
        seed_low,
        seed_high,
        jnp.cos(colatitude)[None, :],
    )


def row_masks(switch, slots, shape):
    source, group = pl.program_id(0), pl.program_id(1)
    lane = lax.broadcasted_iota(jnp.int32, shape, 1)
    masks = []
    for slot in range(SLOTS):
        place = group * SLOTS + slot
        turn = switch[source * slots + place]
        in_low = lane < turn
        even = ((lane - jnp.where(in_low, place, turn)) & 1) == 0
        anchor = (lane == place) & (turn == place + NM)
        masks.append((in_low, even, pl.multiple_of(place * NM, NM), anchor))
    return masks


def mirror_sign(fields):
    lane = lax.broadcasted_iota(jnp.int32, (fields, 128), 1)
    return jnp.where(lane < 64, 1.0, -1.0).astype(F32)


def synthesis_kernel(switch, spec, table, forcing, out, *, slots):
    window = table.shape[1]
    fields = 2 * spec.shape[2]
    sign = mirror_sign(fields)
    collected = []
    force = jnp.broadcast_to(forcing[...], (fields, window))
    masks = row_masks(switch, slots, (fields, window))
    for slot, (in_low, even, start, anchor) in enumerate(masks):
        rows = jnp.concatenate(
            [spec[team, 0, :, pl.ds(start, window)].astype(F32) for team in range(2)], axis=0
        )
        rows = rows + jnp.where(anchor, force, 0.0)
        low, high = jnp.where(in_low, rows, 0.0), jnp.where(in_low, 0.0, rows)
        split = [
            jnp.where(even, low, 0.0),
            jnp.where(even, 0.0, low),
            jnp.where(even, high, 0.0),
            jnp.where(even, 0.0, high),
        ]
        made = jnp.dot(
            jnp.concatenate(split, axis=0).astype(BF16), table[slot], preferred_element_type=F32
        )
        for order in range(2):
            same = made[2 * order * fields : (2 * order + 1) * fields]
            flips = made[(2 * order + 1) * fields : (2 * order + 2) * fields]
            collected.append(
                jnp.concatenate(
                    [
                        same[:, :128] + flips[:, :128],
                        same[:, :128] - flips[:, :128],
                        same[:, 128:] + sign * flips[:, 128:],
                    ],
                    axis=1,
                )
            )
    out[...] = swap_major(jnp.stack(collected)).astype(BF16)


def synthesis(spec, table, forcing, switch, slots):
    _, sources, rows, width = spec.shape
    fields = 2 * rows
    pairs, window, lanes = table.shape
    groups = slots // SLOTS
    return pl.pallas_call(
        functools.partial(synthesis_kernel, slots=slots),
        grid_spec=pltpu.PrefetchScalarGridSpec(
            num_scalar_prefetch=1,
            grid=(sources, groups),
            in_specs=[
                pl.BlockSpec((2, 1, rows, width), lambda z, g, _: (0, z, 0, 0)),
                pl.BlockSpec((SLOTS, window, lanes), lambda z, g, _: (z * groups + g, 0, 0)),
                pl.BlockSpec((fields, 1), lambda z, g, _: (0, 0)),
            ],
            out_specs=pl.BlockSpec(
                (fields, 2 * SLOTS, NLAT), lambda z, g, _: (0, z * groups + g, 0)
            ),
        ),
        out_shape=jax.ShapeDtypeStruct((fields, 2 * pairs, NLAT), BF16),
        compiler_params=pltpu.CompilerParams(vmem_limit_bytes=VMEM_CAP),
        cost_estimate=work(14),
        name="synthesis",
    )(switch, spec, table, forcing)


LON_TILE = 256


def grid_kernel(
    spectra, first, second, arrange, inverse_cos, inverse_sin, forward_cos, forward_sin, weights,
    out, wind, emf,
):
    @pl.when(pl.program_id(0) == 0)
    def _():
        for c in range(3):
            bands = [
                half[z, c] for z in range(first.shape[0]) for half in (first, second)
            ]
            wind[c] = lax.dot_general(
                jnp.concatenate(bands, axis=0),
                arrange[...],
                (((0,), (0,)), ((), ())),
                preferred_element_type=F32,
            ).astype(BF16)

    for tile in range(NLON // LON_TILE):
        span = pl.ds(tile * LON_TILE, LON_TILE)
        magnetic = [
            jnp.dot(inverse_cos[span, :], spectra[2 * c], preferred_element_type=F32)
            + jnp.dot(inverse_sin[span, :], spectra[2 * c + 1], preferred_element_type=F32)
            for c in range(3)
        ]
        motion = [wind[c, span, :].astype(F32) for c in range(3)]
        for c in range(3):
            one, two = (c + 1) % 3, (c + 2) % 3
            emf[c, span, :] = (
                motion[one] * magnetic[two] - motion[two] * magnetic[one]
            ).astype(BF16)
    scale = weights[...]
    for c in range(3):
        for part, table in enumerate((forward_cos, forward_sin)):
            back = jnp.dot(table[...], emf[c], preferred_element_type=F32)
            out[2 * c + part] = (back * scale).astype(BF16)


def grid_product(spectra, first, second, arrange, tables, weights):
    fields, orders, lats = spectra.shape
    whole = lambda array: pl.BlockSpec(array.shape, lambda g: (0,) * array.ndim)
    per_group = pl.BlockSpec((6, orders, lats), lambda g: (g, 0, 0))
    fixed = (first, second, arrange) + tuple(tables) + (weights,)
    return pl.pallas_call(
        grid_kernel,
        grid=(fields // 6,),
        in_specs=[per_group] + [whole(array) for array in fixed],
        out_specs=per_group,
        out_shape=jax.ShapeDtypeStruct(spectra.shape, BF16),
        scratch_shapes=[pltpu.VMEM((3, NLON, lats), BF16)] * 2,
        compiler_params=pltpu.CompilerParams(vmem_limit_bytes=VMEM_CAP),
        cost_estimate=work(16),
        name="grid_product",
    )(spectra, *fixed)


def analysis_kernel(switch, fourier, table, out, carry, *, slots):
    group = pl.program_id(1)
    window = table.shape[1]
    fields = fourier.shape[0]
    half = fields // 2
    sign = mirror_sign(fields)
    by_order = swap_major(fourier[...].astype(F32))

    @pl.when(group == 0)
    def _():
        carry[...] = jnp.zeros_like(carry)

    over = carry[...]
    blank = jnp.zeros((fields, 128 - (window - NM)), F32)
    masks = row_masks(switch, slots, (fields, window))
    for slot, (in_low, even, start, _) in enumerate(masks):
        split = []
        for order in range(2):
            values = by_order[2 * slot + order]
            north, south, rest = values[:, :128], values[:, 128:256], values[:, 256:]
            split += [
                jnp.concatenate([north + south, rest], axis=1),
                jnp.concatenate([north - south, rest * sign], axis=1),
            ]
        made = lax.dot_general(
            jnp.concatenate(split, axis=0).astype(BF16),
            table[slot],
            (((1,), (1,)), ((), ())),
            preferred_element_type=F32,
        )
        part = [made[k * fields : (k + 1) * fields] for k in range(4)]
        rows = jnp.where(
            in_low, jnp.where(even, part[0], part[1]), jnp.where(even, part[2], part[3])
        )
        head = rows[:, :128] + over
        for team in range(2):
            mine = slice(team * half, (team + 1) * half)
            out[team, 0, :, pl.ds(start, 128)] = head[mine].astype(BF16)
            out[team, 0, :, pl.ds(start + 128, NM - 128)] = rows[mine, 128:NM].astype(BF16)
        over = jnp.concatenate([rows[:, NM:], blank], axis=1)
    carry[...] = over

    @pl.when(group == pl.num_programs(1) - 1)
    def _():
        width = out.shape[3]
        full = width // NM * NM
        for team in range(2):
            mine = slice(team * half, (team + 1) * half)
            out[team, 0, :, full:] = over[mine, : width - full].astype(BF16)


def analysis(fourier, table, switch, slots, width):
    fields, orders, lats = fourier.shape
    pairs, window, lanes = table.shape
    groups = slots // SLOTS
    sources = pairs // slots
    return pl.pallas_call(
        functools.partial(analysis_kernel, slots=slots),
        grid_spec=pltpu.PrefetchScalarGridSpec(
            num_scalar_prefetch=1,
            grid=(sources, groups),
            in_specs=[
                pl.BlockSpec((fields, 2 * SLOTS, NLAT), lambda z, g, _: (0, z * groups + g, 0)),
                pl.BlockSpec((SLOTS, window, lanes), lambda z, g, _: (z * groups + g, 0, 0)),
            ],
            out_specs=pl.BlockSpec((2, 1, fields // 2, width), lambda z, g, _: (0, z, 0, 0)),
            scratch_shapes=[pltpu.VMEM((fields, 128), F32)],
        ),
        out_shape=jax.ShapeDtypeStruct((2, sources, fields // 2, width), BF16),
        compiler_params=pltpu.CompilerParams(vmem_limit_bytes=VMEM_CAP),
        cost_estimate=work(14),
        name="analysis",
    )(switch, fourier, table)


def finish_kernel(base, tendency, out):
    fields = tendency.shape[2]
    for field in range(fields):
        out[0, field, :, :, 0] = base[0, field, :, :, 0] + step_weight * tendency[
            :, :, field
        ].astype(F32)


def finish(total, tendency, level):
    tests, comps, teams, count, depth, parts, width = total.shape
    own = pl.BlockSpec(
        (1, comps, teams, count, 1, parts, width), lambda s: (s, 0, 0, 0, level, 0, 0)
    )
    return pl.pallas_call(
        finish_kernel,
        grid=(tests,),
        in_specs=[
            own,
            pl.BlockSpec((teams, count, comps, parts, width), lambda s: (0, 0, s, 0, 0)),
        ],
        out_specs=own,
        out_shape=jax.ShapeDtypeStruct(total.shape, F32),
        input_output_aliases={0: 0},
        compiler_params=pltpu.CompilerParams(vmem_limit_bytes=VMEM_CAP),
        cost_estimate=work(5),
        name="finish",
    )(total, tendency)


def gather_pairs(pair_list, count):
    own = pair_list.shape[0]
    place = lax.axis_index("ma")
    every = jnp.zeros((count, own), jnp.int32)
    every = lax.dynamic_update_slice(every, pair_list[None], (place, 0))
    for shift in range(1, count):
        moved = lax.ppermute(pair_list, "ma", [(k, (k + shift) % count) for k in range(count)])
        every = lax.dynamic_update_slice(every, moved[None], ((place - shift) % count, 0))
    return every.reshape(-1)


def shards_by_level(section, start, velocity, pair_list, wavenumber, *, count):
    slots = pair_list.shape[0]
    width = section.shape[-1]
    depth = LEV // (2 * count)
    band = velocity.shape[0]
    half = band // 2
    place = lax.axis_index("ma")
    across = lax.axis_index("x")
    core = lax.axis_index("k")
    swap_cores = [(0, 1), (1, 0)]
    every_pair = gather_pairs(pair_list, count)
    slot_of = jnp.arange(count * slots, dtype=jnp.int32) % slots
    switch = slot_of + NM - every_pair

    other = lax.ppermute(wavenumber, "k", swap_cores)
    waves_here = jnp.where(core == 0, jnp.stack([wavenumber, other]), jnp.stack([other, wavenumber]))
    forcing = jnp.stack([test_field(waves_here[team, 0], TESTS, LEV) for team in range(2)])
    forcing = forcing.reshape(2 * TESTS * 3, LEV)
    forcing = lax.dynamic_slice_in_dim(forcing, (core * count + place) * depth, depth, axis=1)
    forcing = jnp.stack([forcing, jnp.zeros_like(forcing)], axis=1).reshape(-1, depth)

    bands = velocity.reshape(2, half, 3, LEV // 4, NLON).transpose(0, 3, 2, 1, 4)
    mine = lax.dynamic_index_in_dim(bands, core, 0, keepdims=False)
    theirs = lax.dynamic_index_in_dim(bands, 1 - core, 0, keepdims=False)
    theirs = lax.ppermute(theirs, "k", swap_cores)
    split = jnp.where(core == 0, jnp.stack([mine, theirs]), jnp.stack([theirs, mine]))
    split = split.reshape(count, depth, 3, half, NLON)

    mid = NLAT // 2
    north = jnp.arange(mid, dtype=jnp.int32)
    lats = jnp.concatenate(
        [north[:128], NLAT - 1 - north[:128], north[128:], NLAT - 1 - north[128:]]
    )
    arrange = (jnp.arange(NLAT, dtype=jnp.int32)[:, None] == lats[None, :]).astype(BF16)
    table = legendre_table(every_pair, slots, jnp.concatenate([north, north[128:]]))
    order_list = jnp.stack([every_pair, NM - 1 - every_pair], axis=1).reshape(-1)
    waves = wave_table(order_list, NLON)
    inverse_table = (waves * grid_scale).astype(BF16)
    forward_table = (waves * (2.0 * jnp.pi / NLON)).astype(BF16)
    tables = (inverse_table[0].T, inverse_table[1].T, forward_table[0], forward_table[1])
    weights = lat_weights(lats, NLAT)[None, :]

    row_index = jnp.arange(PAIR_ROWS, dtype=jnp.int32)
    first_half = row_index[None, :] < (NM - pair_list)[:, None]
    degree = jnp.where(first_half, pair_list[:, None] + row_index[None, :], row_index[None, :] - 1)
    spread = (degree * (degree + 1)).astype(F32).reshape(-1)
    total = start[0] - (step_weight * diffusion) * spread * section[0].astype(F32)
    total = total.reshape(TESTS, 3, 2, count, depth, 2, width)

    own_first = (across == 0) & (core == 0)
    own_second = (across == 1) & (core == 1)

    by_level = section.reshape(TESTS * 3, 2 * count, depth, 2, width)
    last = (every_pair,)
    specs, winds = [], []
    for level in range(depth):
        sent = after(by_level[:, :, level].swapaxes(0, 1), *last)
        arrived = lax.all_to_all(sent, ("k", "ma"), split_axis=0, concat_axis=0, tiled=True)
        specs.append(arrived.reshape(2, count, TESTS * 6, width))
        gate = (arrived, table) if level == 0 else (arrived,)
        held = lax.all_to_all(
            after(split[:, level], *gate), "ma", split_axis=0, concat_axis=0, tiled=True
        )
        last = (held,)
        turn = lax.ppermute(held, ("x", "k"), [(0, 2), (1, 0), (2, 3), (3, 1)])
        cross = lax.ppermute(held, ("x", "k"), [(1, 2), (2, 1)])
        first = jnp.where(own_first, held, jnp.where((across == 0) & (core == 1), cross, turn))
        second = jnp.where(own_second, held, jnp.where((across == 1) & (core == 0), cross, turn))
        winds.append((first, second))

    for level in range(depth):
        spectra = synthesis(specs[level], table, forcing[:, level : level + 1], switch, slots)
        fourier = grid_product(spectra, *winds[level], arrange, tables, weights)
        tendency = analysis(fourier, table, switch, slots, width)
        back = after(tendency.reshape(2 * count, TESTS * 3, 2, width), *last)
        back = lax.all_to_all(back, ("k", "ma"), split_axis=0, concat_axis=0, tiled=True)
        last = (back,)
        total = finish(total, back.reshape(2, count, TESTS * 3, 2, width), level)
    return total.reshape(start.shape)


def solution(mesh):
    sizes = dict(mesh.shape)
    count = sizes["ma"]
    whole_slots = (NM // 2) % (count * SLOTS) == 0
    if sizes["team"] == 4 and LEV % (2 * count) == 0 and whole_slots:
        grid = Mesh(
            mesh.devices.reshape(sizes["run"], 2, 2, count), ("run", "x", "k", "ma")
        )
        team = ("x", "k")
        body = lambda *arrays: shards_by_level(*arrays, count=count)
    else:
        grid, team, body = mesh, ("team",), shards_general
    placed = (
        P(("run",) + team, None, None, None, None, "ma"),
        P(("run",) + team, None, None, None, None, "ma"),
        P(("run", "ma"), None, team, None),
        P("ma"),
        P(team),
    )
    return jax.shard_map(
        body,
        mesh=grid,
        in_specs=placed,
        out_specs=P(("run",) + team, None, None, None, None, "ma"),
        check_vma=False,
    )
```

```python
import functools
import math

import jax
import jax.numpy as jnp
from jax import lax
from jax.experimental import pallas as pl
from jax.experimental.pallas import tpu as pltpu
from jax.sharding import Mesh, PartitionSpec as P

NM = 256
NLAT = 384
NLON = 768
LEV = 24
TESTS = 2


grid_scale = 1.0 / 64.0
anchor_gain = 64.0 * math.sqrt(4.0 * math.pi)
quadrature_gain = 64.0
diffusion = 7e-06
step_weight = 2.0
row_block = 16


def seed_values(order_real, order_count, sine_theta):
    factor_index = jnp.arange(1, order_count, dtype=jnp.float32)
    factor_log = jnp.log((2.0 * factor_index - 1.0) / (2.0 * factor_index))
    partial_log = jnp.sum(
        jnp.where(factor_index[None, :] <= order_real[:, None], factor_log[None, :], 0.0), axis=1
    )
    seed_log = 0.5 * (jnp.log((2.0 * order_real + 1.0) / (4.0 * jnp.pi)) + partial_log)
    return jnp.exp(seed_log[:, None] + order_real[:, None] * jnp.log(sine_theta)[None, :])


def pair_table(pair_ids, order_count, lat_count):
    pair_count = pair_ids.shape[0]
    order_low = pair_ids.astype(jnp.float32)
    order_high = (order_count - 1 - pair_ids).astype(jnp.float32)
    colatitude = jnp.pi * (jnp.arange(lat_count, dtype=jnp.float32) + 0.5) / lat_count
    cosine = jnp.cos(colatitude)
    sine_theta = jnp.sin(colatitude)
    seed_low = seed_values(order_low, order_count, sine_theta)
    seed_high = seed_values(order_high, order_count, sine_theta)
    switch_row = order_count - pair_ids

    def one_row(state_pair, row_id):
        latest, before = state_pair
        in_low = row_id < switch_row
        degree = jnp.where(in_low, pair_ids + row_id, row_id - 1)
        order_real = jnp.where(in_low, order_low, order_high)
        degree_real = degree.astype(jnp.float32)
        active = degree_real > order_real
        divisor = jnp.where(active, degree_real * degree_real - order_real * order_real, 1.0)
        upper = jnp.sqrt(jnp.maximum(4.0 * degree_real * degree_real - 1.0, 0.0) / divisor)
        lower_num = ((degree_real - 1.0) * (degree_real - 1.0) - order_real * order_real) * (
            2.0 * degree_real + 1.0
        )
        lower = jnp.sqrt(
            jnp.maximum(lower_num, 0.0) / (divisor * jnp.maximum(2.0 * degree_real - 3.0, 1.0))
        )
        recurred = upper[:, None] * cosine[None, :] * latest - lower[:, None] * before
        is_seed = (row_id == 0) | (row_id == switch_row)
        seeded = jnp.where(in_low[:, None], seed_low, seed_high)
        current = jnp.where(is_seed[:, None], seeded, jnp.where(active[:, None], recurred, 0.0))
        return ((current, latest), current)

    def block_rows(state_pair, first_row):
        produced = []
        for offset in range(row_block):
            state_pair, current = one_row(state_pair, first_row + offset)
            produced.append(current)
        return (state_pair, jnp.stack(produced))

    turns = -(-(order_count + 1) // row_block)
    blank_rows = jnp.zeros((pair_count, lat_count), jnp.float32)
    firsts = jnp.arange(turns, dtype=jnp.int32) * row_block
    _, values = lax.scan(block_rows, (blank_rows, blank_rows), firsts)
    leg_table = values.reshape(turns * row_block, pair_count, lat_count)[: order_count + 1]
    row_index = jnp.arange(order_count + 1, dtype=jnp.int32)
    first_half = row_index[None, :] < (order_count - pair_ids)[:, None]
    degree = jnp.where(first_half, pair_ids[:, None] + row_index[None, :], row_index[None, :] - 1)
    return (leg_table, first_half, degree)


def wave_table(order_list, lon_count):
    longitude = jnp.arange(lon_count, dtype=jnp.int32)
    phase_index = order_list[:, None] * longitude[None, :] % lon_count
    angle_rad = 2.0 * jnp.pi / lon_count * phase_index.astype(jnp.float32)
    return jnp.stack([jnp.cos(angle_rad), jnp.sin(angle_rad)])


def lat_weights(latitudes, lat_count):
    colatitude = jnp.pi * (latitudes.astype(jnp.float32) + 0.5) / lat_count
    return quadrature_gain * (jnp.pi / lat_count) * jnp.sin(colatitude)


def test_field(wave_index, test_count, levels):
    component = jnp.arange(3, dtype=jnp.int32)
    test_ids = jnp.arange(test_count, dtype=jnp.int32)
    level_ids = jnp.arange(levels, dtype=jnp.float32)
    aligned = (component[None, :] == test_ids[:, None]).astype(jnp.float32)
    profile = jnp.cos(jnp.pi * wave_index.astype(jnp.float32) * (level_ids + 0.5) / levels)
    return anchor_gain * aligned[:, :, None] * profile[None, None, :]


def cross_field(motion, magnetic, along):
    return jnp.roll(motion, -1, along) * jnp.roll(magnetic, -2, along) - jnp.roll(
        motion, -2, along
    ) * jnp.roll(magnetic, -1, along)


def shards_general(section, start, velocity, pair_list, wavenumber):
    pair_count = pair_list.shape[0]
    leg_table, first_half, degree = pair_table(pair_list, NM, NLAT)
    legendre = leg_table.astype(jnp.bfloat16)
    selectors = jnp.stack([first_half, jnp.logical_not(first_half)], axis=1)
    masks_low = selectors.astype(jnp.bfloat16)
    anchor = (pair_list == 0)[:, None] & (jnp.arange(NM + 1) == 0)[None, :]
    anchor_rows = anchor.reshape(-1).astype(jnp.float32)
    part_pick = jnp.array([1.0, 0.0], jnp.float32)
    forcing = test_field(wavenumber[0], TESTS, LEV)
    spec_field = (
        section[0].astype(jnp.float32)
        + forcing[:, :, :, None, None] * part_pick[:, None] * anchor_rows[None, :]
    )
    spec_field = spec_field.astype(jnp.bfloat16).reshape(TESTS, 3, LEV, 2, pair_count, NM + 1)
    masked = spec_field[:, :, :, :, :, None, :] * masks_low
    spectra = jnp.einsum(
        "scvpqhr,rqa->ascvpqh", masked, legendre, preferred_element_type=jnp.float32
    )
    spectra = spectra.astype(jnp.bfloat16).reshape(NLAT, TESTS, 3, LEV, 2, 2 * pair_count)
    every_pair = lax.all_gather(pair_list, "ma", axis=0, tiled=True)
    order_list = jnp.stack([every_pair, NM - 1 - every_pair], axis=1).reshape(-1)
    waves = wave_table(order_list, NLON)
    inverse_table = (waves * grid_scale).astype(jnp.bfloat16)
    forward_table = (waves * (2.0 * jnp.pi / NLON)).astype(jnp.bfloat16)
    wind_field = lax.all_gather(velocity, "team", axis=2, tiled=True)
    band_size = velocity.shape[0]
    latitudes = lax.axis_index("ma") * band_size + jnp.arange(band_size, dtype=jnp.int32)
    weights = lat_weights(latitudes, NLAT)
    collected = []
    for test_id in range(TESTS):
        grid_field = jnp.einsum(
            "ascvpm,pmo->ascvo",
            lax.all_to_all(
                spectra[:, test_id : test_id + 1], "ma", split_axis=0, concat_axis=5, tiled=True
            ),
            inverse_table,
            preferred_element_type=jnp.float32,
        )
        emf = cross_field(wind_field[:, None], grid_field, 2).astype(jnp.bfloat16)
        fourier = jnp.einsum(
            "ascvo,pmo->ascvpm", emf, forward_table, preferred_element_type=jnp.float32
        )
        fourier = (fourier * weights[:, None, None, None, None, None]).astype(jnp.bfloat16)
        collected.append(lax.all_to_all(fourier, "ma", split_axis=5, concat_axis=0, tiled=True))
    returned = jnp.concatenate(collected, axis=1)
    returned = returned.reshape(NLAT, TESTS, 3, LEV, 2, pair_count, 2)
    project = jnp.einsum(
        "ascvpqh,rqa->scvpqhr", returned, legendre, preferred_element_type=jnp.float32
    )
    tendency = jnp.sum(project * selectors.astype(jnp.float32), axis=5).reshape(
        TESTS, 3, LEV, 2, -1
    )
    spread = (degree * (degree + 1)).astype(jnp.float32).reshape(-1)
    updated = start[0] + step_weight * (
        tendency - diffusion * spread * section[0].astype(jnp.float32)
    )
    return updated[None]


BF16 = jnp.bfloat16
F32 = jnp.float32
VMEM_CAP = 56 << 20
PAIR_ROWS = NM + 1
CHUNK_ROWS = 16
SLOTS = 8


def work(micros):
    return pl.CostEstimate(
        flops=int(micros * 1e9), transcendentals=0, bytes_accessed=int(micros * 1e6)
    )


def after(value, *others):
    return lax.optimization_barrier((value,) + others)[0]


def table_window(slots):
    return -(-(PAIR_ROWS + slots - 1) // 32) * 32


def swap_major(block):
    return jnp.swapaxes(block, 0, 1)


def table_kernel(upper, lower, first, second, seed_low, seed_high, cosine, out, *, lead):
    shape = seed_low.shape
    cosine_rows = jnp.broadcast_to(cosine[...], shape)
    first_step = first[...]
    second_step = second[...]
    low_value = seed_low[...]
    high_value = seed_high[...]

    def chunk(starting, index, state):
        latest, before = state
        scale_up = upper[index]
        scale_down = lower[index]
        produced = []
        for offset in range(CHUNK_ROWS):
            step = index * CHUNK_ROWS + offset
            current = (scale_up[:, offset : offset + 1] * cosine_rows) * latest - scale_down[
                :, offset : offset + 1
            ] * before
            current = jnp.where(second_step == step, high_value, current)
            if starting:
                current = jnp.where(first_step == step, low_value, current)
            produced.append(current)
            latest, before = current, latest
        rows = swap_major(jnp.stack(produced))
        out[:, pl.ds(pl.multiple_of(index * CHUNK_ROWS, CHUNK_ROWS), CHUNK_ROWS), :] = rows.astype(
            BF16
        )
        return latest, before

    blank = jnp.zeros(shape, F32)
    state = lax.fori_loop(0, lead, functools.partial(chunk, True), (blank, blank))
    lax.fori_loop(lead, out.shape[1] // CHUNK_ROWS, functools.partial(chunk, False), state)


def legendre_table(every_pair, slots, lats):
    pairs = every_pair.shape[0]
    window = table_window(slots)
    order_low = every_pair.astype(F32)
    order_high = (NM - 1 - every_pair).astype(F32)
    colatitude = jnp.pi * (lats.astype(F32) + 0.5) / NLAT
    seed_low = seed_values(order_low, NM, jnp.sin(colatitude))
    seed_high = seed_values(order_high, NM, jnp.sin(colatitude))
    slot = jnp.arange(pairs, dtype=jnp.int32) % slots
    row = jnp.arange(window, dtype=jnp.int32)[None, :] - slot[:, None]
    switch = NM - every_pair
    in_low = row < switch[:, None]
    degree = jnp.where(in_low, every_pair[:, None] + row, row - 1)
    order = jnp.where(in_low, order_low[:, None], order_high[:, None])
    real = degree.astype(F32)
    active = (real > order) & (row >= 0) & (row < PAIR_ROWS)
    divisor = jnp.where(active, real * real - order * order, 1.0)
    upper = jnp.sqrt(jnp.maximum(4.0 * real * real - 1.0, 0.0) / divisor)
    lower_num = ((real - 1.0) * (real - 1.0) - order * order) * (2.0 * real + 1.0)
    lower = jnp.sqrt(
        jnp.maximum(lower_num, 0.0) / (divisor * jnp.maximum(2.0 * real - 3.0, 1.0))
    )
    by_chunk = lambda values: jnp.swapaxes(
        jnp.where(active, values, 0.0).reshape(pairs, window // CHUNK_ROWS, CHUNK_ROWS), 0, 1
    )
    lanes = lats.shape[0]
    spread_out = lambda values: jnp.broadcast_to(values[:, None], (pairs, lanes))
    chunks = window // CHUNK_ROWS
    coefficient = pl.BlockSpec((chunks, 8, CHUNK_ROWS), lambda q: (0, q, 0))
    per_pair = pl.BlockSpec((8, lanes), lambda q: (q, 0))
    lead = -(-slots // CHUNK_ROWS)
    return pl.pallas_call(
        functools.partial(table_kernel, lead=lead),
        grid=(pairs // 8,),
        in_specs=[coefficient, coefficient, per_pair, per_pair, per_pair, per_pair]
        + [pl.BlockSpec((1, lanes), lambda q: (0, 0))],
        out_specs=pl.BlockSpec((8, window, lanes), lambda q: (q, 0, 0)),
        out_shape=jax.ShapeDtypeStruct((pairs, window, lanes), BF16),
        compiler_params=pltpu.CompilerParams(vmem_limit_bytes=VMEM_CAP),
        cost_estimate=work(40),
        name="table",
    )(
        by_chunk(upper),
        by_chunk(lower),
        spread_out(slot),
        spread_out(slot + switch),
        seed_low,
        seed_high,
        jnp.cos(colatitude)[None, :],
    )


def row_mask(switch, source, place, slots, lane):
    turn = switch[source * slots + place]
    in_low = lane < turn
    even = ((lane - jnp.where(in_low, place, turn)) & 1) == 0
    anchor = (lane == place) & (turn == place + NM)
    return in_low, even, anchor


def mirror_sign(fields):
    lane = lax.broadcasted_iota(jnp.int32, (fields, 128), 1)
    return jnp.where(lane < 64, 1.0, -1.0).astype(F32)


def synthesis_kernel(switch, spec, table, forcing, out, *, slots):
    source = pl.program_id(0)
    window = table.shape[1]
    pieces = spec.shape[2]
    fields = 4 * pieces
    sign = mirror_sign(fields)
    lane = lax.broadcasted_iota(jnp.int32, (fields, window), 1)
    force = jnp.broadcast_to(forcing[...], (fields, window))

    def group(index, _):
        collected = []
        for slot in range(SLOTS):
            place = index * SLOTS + slot
            in_low, even, anchor = row_mask(switch, source, place, slots, lane)
            span = pl.ds(pl.multiple_of(place * NM, NM), window)
            rows = jnp.concatenate(
                [
                    spec[team, 0, piece, :, span].astype(F32)
                    for team in range(2)
                    for piece in range(pieces)
                ],
                axis=0,
            )
            rows = rows + jnp.where(anchor, force, 0.0)
            low, high = jnp.where(in_low, rows, 0.0), jnp.where(in_low, 0.0, rows)
            split = [
                jnp.where(even, low, 0.0),
                jnp.where(even, 0.0, low),
                jnp.where(even, high, 0.0),
                jnp.where(even, 0.0, high),
            ]
            made = jnp.dot(
                jnp.concatenate(split, axis=0).astype(BF16),
                table[place],
                preferred_element_type=F32,
            )
            for order in range(2):
                same = made[2 * order * fields : (2 * order + 1) * fields]
                flips = made[(2 * order + 1) * fields : (2 * order + 2) * fields]
                collected.append(
                    jnp.concatenate(
                        [
                            same[:, :128] + flips[:, :128],
                            same[:, :128] - flips[:, :128],
                            same[:, 128:] + sign * flips[:, 128:],
                        ],
                        axis=1,
                    )
                )
        rows = pl.ds(pl.multiple_of(index * 2 * SLOTS, 2 * SLOTS), 2 * SLOTS)
        out[:, rows, :] = swap_major(jnp.stack(collected)).astype(BF16)
        return 0

    lax.fori_loop(0, slots // SLOTS, group, 0)


def synthesis(spec, table, forcing, switch, slots):
    _, sources, pieces, parts, width = spec.shape
    fields = 2 * pieces * parts
    pairs, window, lanes = table.shape
    return pl.pallas_call(
        functools.partial(synthesis_kernel, slots=slots),
        grid_spec=pltpu.PrefetchScalarGridSpec(
            num_scalar_prefetch=1,
            grid=(sources,),
            in_specs=[
                pl.BlockSpec((2, 1, pieces, parts, width), lambda z, _: (0, z, 0, 0, 0)),
                pl.BlockSpec((slots, window, lanes), lambda z, _: (z, 0, 0)),
                pl.BlockSpec((fields, 1), lambda z, _: (0, 0)),
            ],
            out_specs=pl.BlockSpec((fields, 2 * slots, NLAT), lambda z, _: (0, z, 0)),
        ),
        out_shape=jax.ShapeDtypeStruct((fields, 2 * pairs, NLAT), BF16),
        compiler_params=pltpu.CompilerParams(vmem_limit_bytes=VMEM_CAP),
        cost_estimate=work(14),
        name="synthesis",
    )(switch, spec, table, forcing)


LON_TILE = 256


def grid_kernel(
    spectra, first, second, arrange, inverse_cos, inverse_sin, forward_cos, forward_sin, weights,
    out, wind, emf,
):
    @pl.when(pl.program_id(0) == 0)
    def _():
        for c in range(3):
            bands = [
                half[z, c] for z in range(first.shape[0]) for half in (first, second)
            ]
            wind[c] = lax.dot_general(
                jnp.concatenate(bands, axis=0),
                arrange[...],
                (((0,), (0,)), ((), ())),
                preferred_element_type=F32,
            ).astype(BF16)

    for tile in range(NLON // LON_TILE):
        span = pl.ds(tile * LON_TILE, LON_TILE)
        magnetic = [
            jnp.dot(inverse_cos[span, :], spectra[2 * c], preferred_element_type=F32)
            + jnp.dot(inverse_sin[span, :], spectra[2 * c + 1], preferred_element_type=F32)
            for c in range(3)
        ]
        motion = [wind[c, span, :].astype(F32) for c in range(3)]
        for c in range(3):
            one, two = (c + 1) % 3, (c + 2) % 3
            emf[c, span, :] = (
                motion[one] * magnetic[two] - motion[two] * magnetic[one]
            ).astype(BF16)
    scale = weights[...]
    for c in range(3):
        for part, table in enumerate((forward_cos, forward_sin)):
            back = jnp.dot(table[...], emf[c], preferred_element_type=F32)
            out[2 * c + part] = (back * scale).astype(BF16)


def grid_product(spectra, first, second, arrange, tables, weights):
    fields, orders, lats = spectra.shape
    whole = lambda array: pl.BlockSpec(array.shape, lambda g: (0,) * array.ndim)
    per_group = pl.BlockSpec((6, orders, lats), lambda g: (g, 0, 0))
    fixed = (first, second, arrange) + tuple(tables) + (weights,)
    return pl.pallas_call(
        grid_kernel,
        grid=(fields // 6,),
        in_specs=[per_group] + [whole(array) for array in fixed],
        out_specs=per_group,
        out_shape=jax.ShapeDtypeStruct(spectra.shape, BF16),
        scratch_shapes=[pltpu.VMEM((3, NLON, lats), BF16)] * 2,
        compiler_params=pltpu.CompilerParams(vmem_limit_bytes=VMEM_CAP),
        cost_estimate=work(16),
        name="grid_product",
    )(spectra, *fixed)


def analysis_kernel(switch, fourier, table, out, *, slots):
    source = pl.program_id(0)
    window = table.shape[1]
    fields = fourier.shape[0]
    pieces = out.shape[2]
    width = out.shape[4]
    sign = mirror_sign(fields)
    lane = lax.broadcasted_iota(jnp.int32, (fields, window), 1)
    blank = jnp.zeros((fields, 128 - (window - NM)), F32)

    def store(values, span):
        for team in range(2):
            for piece in range(pieces):
                row = 2 * (team * pieces + piece)
                out[team, 0, piece, :, span] = values[row : row + 2].astype(BF16)

    def group(index, over):
        rows = pl.ds(pl.multiple_of(index * 2 * SLOTS, 2 * SLOTS), 2 * SLOTS)
        by_order = swap_major(fourier[:, rows, :].astype(F32))
        for slot in range(SLOTS):
            place = index * SLOTS + slot
            in_low, even, _ = row_mask(switch, source, place, slots, lane)
            split = []
            for order in range(2):
                values = by_order[2 * slot + order]
                north, south, rest = values[:, :128], values[:, 128:256], values[:, 256:]
                split += [
                    jnp.concatenate([north + south, rest], axis=1),
                    jnp.concatenate([north - south, rest * sign], axis=1),
                ]
            made = lax.dot_general(
                jnp.concatenate(split, axis=0).astype(BF16),
                table[place],
                (((1,), (1,)), ((), ())),
                preferred_element_type=F32,
            )
            part = [made[k * fields : (k + 1) * fields] for k in range(4)]
            made = jnp.where(
                in_low, jnp.where(even, part[0], part[1]), jnp.where(even, part[2], part[3])
            )
            start = pl.multiple_of(place * NM, NM)
            store(
                jnp.concatenate([made[:, :128] + over, made[:, 128:NM]], axis=1),
                pl.ds(start, NM),
            )
            over = jnp.concatenate([made[:, NM:], blank], axis=1)
        return over

    over = lax.fori_loop(0, slots // SLOTS, group, jnp.zeros((fields, 128), F32))
    full = slots * NM
    store(over[:, : width - full], pl.ds(full, width - full))


def analysis(fourier, table, switch, slots, width):
    fields, orders, lats = fourier.shape
    pairs, window, lanes = table.shape
    sources = pairs // slots
    pieces = fields // 4
    return pl.pallas_call(
        functools.partial(analysis_kernel, slots=slots),
        grid_spec=pltpu.PrefetchScalarGridSpec(
            num_scalar_prefetch=1,
            grid=(sources,),
            in_specs=[
                pl.BlockSpec((fields, 2 * slots, NLAT), lambda z, _: (0, z, 0)),
                pl.BlockSpec((slots, window, lanes), lambda z, _: (z, 0, 0)),
            ],
            out_specs=pl.BlockSpec((2, 1, pieces, 2, width), lambda z, _: (0, z, 0, 0, 0)),
        ),
        out_shape=jax.ShapeDtypeStruct((2, sources, pieces, 2, width), BF16),
        compiler_params=pltpu.CompilerParams(vmem_limit_bytes=VMEM_CAP),
        cost_estimate=work(14),
        name="analysis",
    )(switch, fourier, table)


def pack_kernel(section, out):
    out[0] = section[:, 0, 0]


def pack_level(section, level):
    pieces, targets, _, parts, width = section.shape
    return pl.pallas_call(
        pack_kernel,
        grid=(targets,),
        in_specs=[pl.BlockSpec((pieces, 1, 1, parts, width), lambda d: (0, d, level, 0, 0))],
        out_specs=pl.BlockSpec((1, pieces, parts, width), lambda d: (d, 0, 0, 0)),
        out_shape=jax.ShapeDtypeStruct((targets, pieces, parts, width), BF16),
        cost_estimate=work(5),
        name="pack",
    )(section)


def finish_kernel(base, tendency, out):
    fields = tendency.shape[2]
    for field in range(fields):
        out[0, field, :, :, 0] = base[0, field, :, :, 0] + step_weight * tendency[
            :, :, field
        ].astype(F32)


def finish(total, tendency, level):
    tests, comps, teams, count, depth, parts, width = total.shape
    own = pl.BlockSpec(
        (1, comps, teams, count, 1, parts, width), lambda s: (s, 0, 0, 0, level, 0, 0)
    )
    return pl.pallas_call(
        finish_kernel,
        grid=(tests,),
        in_specs=[
            own,
            pl.BlockSpec((teams, count, comps, parts, width), lambda s: (0, 0, s, 0, 0)),
        ],
        out_specs=own,
        out_shape=jax.ShapeDtypeStruct(total.shape, F32),
        input_output_aliases={0: 0},
        compiler_params=pltpu.CompilerParams(vmem_limit_bytes=VMEM_CAP),
        cost_estimate=work(5),
        name="finish",
    )(total, tendency)


def gather_pairs(pair_list, count):
    own = pair_list.shape[0]
    place = lax.axis_index("ma")
    every = jnp.zeros((count, own), jnp.int32)
    every = lax.dynamic_update_slice(every, pair_list[None], (place, 0))
    for shift in range(1, count):
        moved = lax.ppermute(pair_list, "ma", [(k, (k + shift) % count) for k in range(count)])
        every = lax.dynamic_update_slice(every, moved[None], ((place - shift) % count, 0))
    return every.reshape(-1)


def shards_by_level(section, start, velocity, pair_list, wavenumber, *, count):
    slots = pair_list.shape[0]
    width = section.shape[-1]
    depth = LEV // (2 * count)
    band = velocity.shape[0]
    half = band // 2
    place = lax.axis_index("ma")
    across = lax.axis_index("x")
    core = lax.axis_index("k")
    swap_cores = [(0, 1), (1, 0)]
    every_pair = gather_pairs(pair_list, count)
    slot_of = jnp.arange(count * slots, dtype=jnp.int32) % slots
    switch = slot_of + NM - every_pair

    other = lax.ppermute(wavenumber, "k", swap_cores)
    waves_here = jnp.where(core == 0, jnp.stack([wavenumber, other]), jnp.stack([other, wavenumber]))
    forcing = jnp.stack([test_field(waves_here[team, 0], TESTS, LEV) for team in range(2)])
    forcing = forcing.reshape(2 * TESTS * 3, LEV)
    forcing = lax.dynamic_slice_in_dim(forcing, (core * count + place) * depth, depth, axis=1)
    forcing = jnp.stack([forcing, jnp.zeros_like(forcing)], axis=1).reshape(-1, depth)

    by_level = section.reshape(TESTS * 3, 2 * count, depth, 2, width)
    exchange = functools.partial(
        lax.all_to_all, axis_name=("k", "ma"), split_axis=0, concat_axis=0, tiled=True
    )
    sent = pack_level(by_level, 0)
    arrived = exchange(sent)
    specs = [arrived]

    bands = after(velocity, sent).reshape(2, half, 3, LEV // 4, NLON).transpose(0, 3, 2, 1, 4)
    mine = lax.dynamic_index_in_dim(bands, core, 0, keepdims=False)
    theirs = lax.dynamic_index_in_dim(bands, 1 - core, 0, keepdims=False)
    theirs = lax.ppermute(theirs, "k", swap_cores)
    split = jnp.where(core == 0, jnp.stack([mine, theirs]), jnp.stack([theirs, mine]))
    split = split.reshape(count, depth, 3, half, NLON)

    mid = NLAT // 2
    north = jnp.arange(mid, dtype=jnp.int32)
    lats = jnp.concatenate(
        [north[:128], NLAT - 1 - north[:128], north[128:], NLAT - 1 - north[128:]]
    )
    arrange = (jnp.arange(NLAT, dtype=jnp.int32)[:, None] == lats[None, :]).astype(BF16)
    table = legendre_table(every_pair, slots, jnp.concatenate([north, north[128:]]))
    order_list = jnp.stack([every_pair, NM - 1 - every_pair], axis=1).reshape(-1)
    waves = wave_table(order_list, NLON)
    inverse_table = (waves * grid_scale).astype(BF16)
    forward_table = (waves * (2.0 * jnp.pi / NLON)).astype(BF16)
    tables = (inverse_table[0].T, inverse_table[1].T, forward_table[0], forward_table[1])
    weights = lat_weights(lats, NLAT)[None, :]

    row_index = jnp.arange(PAIR_ROWS, dtype=jnp.int32)
    first_half = row_index[None, :] < (NM - pair_list)[:, None]
    degree = jnp.where(first_half, pair_list[:, None] + row_index[None, :], row_index[None, :] - 1)
    spread = (degree * (degree + 1)).astype(F32).reshape(-1)
    total = start[0] - (step_weight * diffusion) * spread * section[0].astype(F32)
    total = total.reshape(TESTS, 3, 2, count, depth, 2, width)

    own_first = (across == 0) & (core == 0)
    own_second = (across == 1) & (core == 1)

    held = lax.all_to_all(
        after(split, arrived, table), "ma", split_axis=0, concat_axis=0, tiled=True
    )
    winds = []
    last = ()
    for group in (slice(0, 1), slice(1, depth)):
        part = after(held[:, group], *last)
        turn = lax.ppermute(part, ("x", "k"), [(0, 2), (1, 0), (2, 3), (3, 1)])
        cross = lax.ppermute(part, ("x", "k"), [(1, 2), (2, 1)])
        first = jnp.where(own_first, part, jnp.where((across == 0) & (core == 1), cross, turn))
        second = jnp.where(own_second, part, jnp.where((across == 1) & (core == 0), cross, turn))
        winds += [(first[:, k], second[:, k]) for k in range(first.shape[1])]
        last = (turn, cross)

    last = (held,)
    for level in range(1, depth):
        specs.append(exchange(after(pack_level(by_level, level), *last)))
        last = (specs[-1],)
    specs = [spec.reshape(2, count, TESTS * 3, 2, width) for spec in specs]

    for level in range(depth):
        spectra = synthesis(specs[level], table, forcing[:, level : level + 1], switch, slots)
        fourier = grid_product(spectra, *winds[level], arrange, tables, weights)
        tendency = analysis(fourier, table, switch, slots, width)
        back = exchange(after(tendency.reshape(2 * count, TESTS * 3, 2, width), *last))
        last = (back,)
        total = finish(total, back.reshape(2, count, TESTS * 3, 2, width), level)
    return total.reshape(start.shape)


def solution(mesh):
    sizes = dict(mesh.shape)
    count = sizes["ma"]
    whole_slots = (NM // 2) % (count * SLOTS) == 0
    if sizes["team"] == 4 and LEV % (2 * count) == 0 and whole_slots:
        grid = Mesh(
            mesh.devices.reshape(sizes["run"], 2, 2, count), ("run", "x", "k", "ma")
        )
        team = ("x", "k")
        body = lambda *arrays: shards_by_level(*arrays, count=count)
    else:
        grid, team, body = mesh, ("team",), shards_general
    placed = (
        P(("run",) + team, None, None, None, None, "ma"),
        P(("run",) + team, None, None, None, None, "ma"),
        P(("run", "ma"), None, team, None),
        P("ma"),
        P(team),
    )
    return jax.shard_map(
        body,
        mesh=grid,
        in_specs=placed,
        out_specs=P(("run",) + team, None, None, None, None, "ma"),
        check_vma=False,
    )
```

```python
import functools
import math

import jax
import jax.numpy as jnp
from jax import lax
from jax.experimental import pallas as pl
from jax.experimental.pallas import tpu as pltpu
from jax.sharding import Mesh, PartitionSpec as P

NM = 256
NLAT = 384
NLON = 768
LEV = 24
TESTS = 2


grid_scale = 1.0 / 64.0
anchor_gain = 64.0 * math.sqrt(4.0 * math.pi)
quadrature_gain = 64.0
diffusion = 7e-06
step_weight = 2.0
row_block = 16


def seed_values(order_real, order_count, sine_theta):
    factor_index = jnp.arange(1, order_count, dtype=jnp.float32)
    factor_log = jnp.log((2.0 * factor_index - 1.0) / (2.0 * factor_index))
    partial_log = jnp.sum(
        jnp.where(factor_index[None, :] <= order_real[:, None], factor_log[None, :], 0.0), axis=1
    )
    seed_log = 0.5 * (jnp.log((2.0 * order_real + 1.0) / (4.0 * jnp.pi)) + partial_log)
    return jnp.exp(seed_log[:, None] + order_real[:, None] * jnp.log(sine_theta)[None, :])


def pair_table(pair_ids, order_count, lat_count):
    pair_count = pair_ids.shape[0]
    order_low = pair_ids.astype(jnp.float32)
    order_high = (order_count - 1 - pair_ids).astype(jnp.float32)
    colatitude = jnp.pi * (jnp.arange(lat_count, dtype=jnp.float32) + 0.5) / lat_count
    cosine = jnp.cos(colatitude)
    sine_theta = jnp.sin(colatitude)
    seed_low = seed_values(order_low, order_count, sine_theta)
    seed_high = seed_values(order_high, order_count, sine_theta)
    switch_row = order_count - pair_ids

    def one_row(state_pair, row_id):
        latest, before = state_pair
        in_low = row_id < switch_row
        degree = jnp.where(in_low, pair_ids + row_id, row_id - 1)
        order_real = jnp.where(in_low, order_low, order_high)
        degree_real = degree.astype(jnp.float32)
        active = degree_real > order_real
        divisor = jnp.where(active, degree_real * degree_real - order_real * order_real, 1.0)
        upper = jnp.sqrt(jnp.maximum(4.0 * degree_real * degree_real - 1.0, 0.0) / divisor)
        lower_num = ((degree_real - 1.0) * (degree_real - 1.0) - order_real * order_real) * (
            2.0 * degree_real + 1.0
        )
        lower = jnp.sqrt(
            jnp.maximum(lower_num, 0.0) / (divisor * jnp.maximum(2.0 * degree_real - 3.0, 1.0))
        )
        recurred = upper[:, None] * cosine[None, :] * latest - lower[:, None] * before
        is_seed = (row_id == 0) | (row_id == switch_row)
        seeded = jnp.where(in_low[:, None], seed_low, seed_high)
        current = jnp.where(is_seed[:, None], seeded, jnp.where(active[:, None], recurred, 0.0))
        return ((current, latest), current)

    def block_rows(state_pair, first_row):
        produced = []
        for offset in range(row_block):
            state_pair, current = one_row(state_pair, first_row + offset)
            produced.append(current)
        return (state_pair, jnp.stack(produced))

    turns = -(-(order_count + 1) // row_block)
    blank_rows = jnp.zeros((pair_count, lat_count), jnp.float32)
    firsts = jnp.arange(turns, dtype=jnp.int32) * row_block
    _, values = lax.scan(block_rows, (blank_rows, blank_rows), firsts)
    leg_table = values.reshape(turns * row_block, pair_count, lat_count)[: order_count + 1]
    row_index = jnp.arange(order_count + 1, dtype=jnp.int32)
    first_half = row_index[None, :] < (order_count - pair_ids)[:, None]
    degree = jnp.where(first_half, pair_ids[:, None] + row_index[None, :], row_index[None, :] - 1)
    return (leg_table, first_half, degree)


def wave_table(order_list, lon_count):
    longitude = jnp.arange(lon_count, dtype=jnp.int32)
    phase_index = order_list[:, None] * longitude[None, :] % lon_count
    angle_rad = 2.0 * jnp.pi / lon_count * phase_index.astype(jnp.float32)
    return jnp.stack([jnp.cos(angle_rad), jnp.sin(angle_rad)])


def lat_weights(latitudes, lat_count):
    colatitude = jnp.pi * (latitudes.astype(jnp.float32) + 0.5) / lat_count
    return quadrature_gain * (jnp.pi / lat_count) * jnp.sin(colatitude)


def test_field(wave_index, test_count, levels):
    component = jnp.arange(3, dtype=jnp.int32)
    test_ids = jnp.arange(test_count, dtype=jnp.int32)
    level_ids = jnp.arange(levels, dtype=jnp.float32)
    aligned = (component[None, :] == test_ids[:, None]).astype(jnp.float32)
    profile = jnp.cos(jnp.pi * wave_index.astype(jnp.float32) * (level_ids + 0.5) / levels)
    return anchor_gain * aligned[:, :, None] * profile[None, None, :]


def cross_field(motion, magnetic, along):
    return jnp.roll(motion, -1, along) * jnp.roll(magnetic, -2, along) - jnp.roll(
        motion, -2, along
    ) * jnp.roll(magnetic, -1, along)


def shards_general(section, start, velocity, pair_list, wavenumber):
    pair_count = pair_list.shape[0]
    leg_table, first_half, degree = pair_table(pair_list, NM, NLAT)
    legendre = leg_table.astype(jnp.bfloat16)
    selectors = jnp.stack([first_half, jnp.logical_not(first_half)], axis=1)
    masks_low = selectors.astype(jnp.bfloat16)
    anchor = (pair_list == 0)[:, None] & (jnp.arange(NM + 1) == 0)[None, :]
    anchor_rows = anchor.reshape(-1).astype(jnp.float32)
    part_pick = jnp.array([1.0, 0.0], jnp.float32)
    forcing = test_field(wavenumber[0], TESTS, LEV)
    spec_field = (
        section[0].astype(jnp.float32)
        + forcing[:, :, :, None, None] * part_pick[:, None] * anchor_rows[None, :]
    )
    spec_field = spec_field.astype(jnp.bfloat16).reshape(TESTS, 3, LEV, 2, pair_count, NM + 1)
    masked = spec_field[:, :, :, :, :, None, :] * masks_low
    spectra = jnp.einsum(
        "scvpqhr,rqa->ascvpqh", masked, legendre, preferred_element_type=jnp.float32
    )
    spectra = spectra.astype(jnp.bfloat16).reshape(NLAT, TESTS, 3, LEV, 2, 2 * pair_count)
    every_pair = lax.all_gather(pair_list, "ma", axis=0, tiled=True)
    order_list = jnp.stack([every_pair, NM - 1 - every_pair], axis=1).reshape(-1)
    waves = wave_table(order_list, NLON)
    inverse_table = (waves * grid_scale).astype(jnp.bfloat16)
    forward_table = (waves * (2.0 * jnp.pi / NLON)).astype(jnp.bfloat16)
    wind_field = lax.all_gather(velocity, "team", axis=2, tiled=True)
    band_size = velocity.shape[0]
    latitudes = lax.axis_index("ma") * band_size + jnp.arange(band_size, dtype=jnp.int32)
    weights = lat_weights(latitudes, NLAT)
    collected = []
    for test_id in range(TESTS):
        grid_field = jnp.einsum(
            "ascvpm,pmo->ascvo",
            lax.all_to_all(
                spectra[:, test_id : test_id + 1], "ma", split_axis=0, concat_axis=5, tiled=True
            ),
            inverse_table,
            preferred_element_type=jnp.float32,
        )
        emf = cross_field(wind_field[:, None], grid_field, 2).astype(jnp.bfloat16)
        fourier = jnp.einsum(
            "ascvo,pmo->ascvpm", emf, forward_table, preferred_element_type=jnp.float32
        )
        fourier = (fourier * weights[:, None, None, None, None, None]).astype(jnp.bfloat16)
        collected.append(lax.all_to_all(fourier, "ma", split_axis=5, concat_axis=0, tiled=True))
    returned = jnp.concatenate(collected, axis=1)
    returned = returned.reshape(NLAT, TESTS, 3, LEV, 2, pair_count, 2)
    project = jnp.einsum(
        "ascvpqh,rqa->scvpqhr", returned, legendre, preferred_element_type=jnp.float32
    )
    tendency = jnp.sum(project * selectors.astype(jnp.float32), axis=5).reshape(
        TESTS, 3, LEV, 2, -1
    )
    spread = (degree * (degree + 1)).astype(jnp.float32).reshape(-1)
    updated = start[0] + step_weight * (
        tendency - diffusion * spread * section[0].astype(jnp.float32)
    )
    return updated[None]


BF16 = jnp.bfloat16
F32 = jnp.float32
VMEM_CAP = 56 << 20
PAIR_ROWS = NM + 1
CHUNK_ROWS = 16
TABLE_PAIRS = 16
SLOTS = 8


def work(micros):
    return pl.CostEstimate(
        flops=int(micros * 1e9), transcendentals=0, bytes_accessed=int(micros * 1e6)
    )


def after(value, *others):
    return lax.optimization_barrier((value,) + others)[0]


def table_window(slots):
    return -(-(PAIR_ROWS + slots - 1) // 32) * 32


def swap_major(block):
    return jnp.swapaxes(block, 0, 1)


def table_kernel(upper, lower, first, second, seed_low, seed_high, cosine, _, out, *, lead):
    shape = seed_low.shape
    cosine_rows = jnp.broadcast_to(cosine[...], shape)
    first_step = first[...]
    second_step = second[...]
    low_value = seed_low[...]
    high_value = seed_high[...]

    def chunk(starting, index, state):
        latest, before = state
        scale_up = upper[index]
        scale_down = lower[index]
        produced = []
        for offset in range(CHUNK_ROWS):
            step = index * CHUNK_ROWS + offset
            current = (scale_up[:, offset : offset + 1] * cosine_rows) * latest - scale_down[
                :, offset : offset + 1
            ] * before
            current = jnp.where(second_step == step, high_value, current)
            if starting:
                current = jnp.where(first_step == step, low_value, current)
            produced.append(current)
            latest, before = current, latest
        rows = swap_major(jnp.stack(produced))
        out[:, pl.ds(pl.multiple_of(index * CHUNK_ROWS, CHUNK_ROWS), CHUNK_ROWS), :] = rows.astype(
            BF16
        )
        return latest, before

    blank = jnp.zeros(shape, F32)
    state = lax.fori_loop(0, lead, functools.partial(chunk, True), (blank, blank))
    lax.fori_loop(lead, out.shape[1] // CHUNK_ROWS, functools.partial(chunk, False), state)


def legendre_table(every_pair, slots, lats):
    pairs = every_pair.shape[0]
    window = table_window(slots)
    order_low = every_pair.astype(F32)
    order_high = (NM - 1 - every_pair).astype(F32)
    colatitude = jnp.pi * (lats.astype(F32) + 0.5) / NLAT
    seed_low = seed_values(order_low, NM, jnp.sin(colatitude))
    seed_high = seed_values(order_high, NM, jnp.sin(colatitude))
    slot = jnp.arange(pairs, dtype=jnp.int32) % slots
    row = jnp.arange(window, dtype=jnp.int32)[None, :] - slot[:, None]
    switch = NM - every_pair
    in_low = row < switch[:, None]
    degree = jnp.where(in_low, every_pair[:, None] + row, row - 1)
    order = jnp.where(in_low, order_low[:, None], order_high[:, None])
    real = degree.astype(F32)
    active = (real > order) & (row >= 0) & (row < PAIR_ROWS)
    divisor = jnp.where(active, real * real - order * order, 1.0)
    upper = jnp.sqrt(jnp.maximum(4.0 * real * real - 1.0, 0.0) / divisor)
    lower_num = ((real - 1.0) * (real - 1.0) - order * order) * (2.0 * real + 1.0)
    lower = jnp.sqrt(
        jnp.maximum(lower_num, 0.0) / (divisor * jnp.maximum(2.0 * real - 3.0, 1.0))
    )
    by_chunk = lambda values: jnp.swapaxes(
        jnp.where(active, values, 0.0).reshape(pairs, window // CHUNK_ROWS, CHUNK_ROWS), 0, 1
    )
    lanes = lats.shape[0]
    spread_out = lambda values: jnp.broadcast_to(values[:, None], (pairs, lanes))
    chunks = window // CHUNK_ROWS
    operands = (
        by_chunk(upper),
        by_chunk(lower),
        spread_out(slot),
        spread_out(slot + switch),
        seed_low,
        seed_high,
        jnp.cos(colatitude)[None, :],
    )
    blocks = pairs // TABLE_PAIRS
    shape = jax.ShapeDtypeStruct((pairs, window, lanes), BF16)
    halves = []
    for begin, end in ((0, blocks // 2), (blocks // 2, blocks)):
        place = lambda q, begin=begin: q + begin
        coefficient = pl.BlockSpec(
            (chunks, TABLE_PAIRS, CHUNK_ROWS), lambda q, place=place: (0, place(q), 0)
        )
        per_pair = pl.BlockSpec((TABLE_PAIRS, lanes), lambda q, place=place: (place(q), 0))
        before = halves[-1:] or [jnp.zeros((8, 128), BF16)]
        halves.append(
            pl.pallas_call(
                functools.partial(table_kernel, lead=-(-slots // CHUNK_ROWS)),
                grid=(end - begin,),
                in_specs=[coefficient, coefficient, per_pair, per_pair, per_pair, per_pair]
                + [pl.BlockSpec((1, lanes), lambda q: (0, 0))]
                + [pl.BlockSpec(memory_space=pl.ANY)],
                out_specs=pl.BlockSpec(
                    (TABLE_PAIRS, window, lanes), lambda q, place=place: (place(q), 0, 0)
                ),
                out_shape=shape,
                input_output_aliases={7: 0} if halves else {},
                compiler_params=pltpu.CompilerParams(vmem_limit_bytes=VMEM_CAP),
                cost_estimate=work(20),
                name="table",
            )(*operands, *before)
        )
    return halves


def row_mask(switch, source, place, slots, lane):
    turn = switch[source * slots + place]
    in_low = lane < turn
    even = ((lane - jnp.where(in_low, place, turn)) & 1) == 0
    anchor = (lane == place) & (turn == place + NM)
    return in_low, even, anchor


def mirror_sign(fields):
    lane = lax.broadcasted_iota(jnp.int32, (fields, 128), 1)
    return jnp.where(lane < 64, 1.0, -1.0).astype(F32)


def synthesis_kernel(switch, spec, table, forcing, out, *, slots):
    source = pl.program_id(0)
    window = table.shape[1]
    pieces = spec.shape[2]
    fields = 4 * pieces
    sign = mirror_sign(fields)
    lane = lax.broadcasted_iota(jnp.int32, (fields, window), 1)
    force = jnp.broadcast_to(forcing[...], (fields, window))

    def group(index, _):
        collected = []
        for slot in range(SLOTS):
            place = index * SLOTS + slot
            in_low, even, anchor = row_mask(switch, source, place, slots, lane)
            span = pl.ds(pl.multiple_of(place * NM, NM), window)
            rows = jnp.concatenate(
                [
                    spec[team, 0, piece, :, span].astype(F32)
                    for team in range(2)
                    for piece in range(pieces)
                ],
                axis=0,
            )
            rows = rows + jnp.where(anchor, force, 0.0)
            low, high = jnp.where(in_low, rows, 0.0), jnp.where(in_low, 0.0, rows)
            split = [
                jnp.where(even, low, 0.0),
                jnp.where(even, 0.0, low),
                jnp.where(even, high, 0.0),
                jnp.where(even, 0.0, high),
            ]
            made = jnp.dot(
                jnp.concatenate(split, axis=0).astype(BF16),
                table[place],
                preferred_element_type=F32,
            )
            for order in range(2):
                same = made[2 * order * fields : (2 * order + 1) * fields]
                flips = made[(2 * order + 1) * fields : (2 * order + 2) * fields]
                collected.append(
                    jnp.concatenate(
                        [
                            same[:, :128] + flips[:, :128],
                            same[:, :128] - flips[:, :128],
                            same[:, 128:] + sign * flips[:, 128:],
                        ],
                        axis=1,
                    )
                )
        rows = pl.ds(pl.multiple_of(index * 2 * SLOTS, 2 * SLOTS), 2 * SLOTS)
        out[:, rows, :] = swap_major(jnp.stack(collected)).astype(BF16)
        return 0

    lax.fori_loop(0, slots // SLOTS, group, 0)


def synthesis(spec, table, forcing, switch, slots):
    _, sources, pieces, parts, width = spec.shape
    fields = 2 * pieces * parts
    pairs, window, lanes = table.shape
    return pl.pallas_call(
        functools.partial(synthesis_kernel, slots=slots),
        grid_spec=pltpu.PrefetchScalarGridSpec(
            num_scalar_prefetch=1,
            grid=(sources,),
            in_specs=[
                pl.BlockSpec((2, 1, pieces, parts, width), lambda z, _: (0, z, 0, 0, 0)),
                pl.BlockSpec((slots, window, lanes), lambda z, _: (z, 0, 0)),
                pl.BlockSpec((fields, 1), lambda z, _: (0, 0)),
            ],
            out_specs=pl.BlockSpec((fields, 2 * slots, NLAT), lambda z, _: (0, z, 0)),
        ),
        out_shape=jax.ShapeDtypeStruct((fields, 2 * pairs, NLAT), BF16),
        compiler_params=pltpu.CompilerParams(vmem_limit_bytes=VMEM_CAP),
        cost_estimate=work(14),
        name="synthesis",
    )(switch, spec, table, forcing)


LON_TILE = 256


def grid_kernel(
    spectra, first, second, arrange, inverse_cos, inverse_sin, forward_cos, forward_sin, weights,
    out, wind, emf,
):
    @pl.when(pl.program_id(0) == 0)
    def _():
        for c in range(3):
            bands = [
                half[z, c] for z in range(first.shape[0]) for half in (first, second)
            ]
            wind[c] = lax.dot_general(
                jnp.concatenate(bands, axis=0),
                arrange[...],
                (((0,), (0,)), ((), ())),
                preferred_element_type=F32,
            ).astype(BF16)

    for tile in range(NLON // LON_TILE):
        span = pl.ds(tile * LON_TILE, LON_TILE)
        magnetic = [
            jnp.dot(inverse_cos[span, :], spectra[2 * c], preferred_element_type=F32)
            + jnp.dot(inverse_sin[span, :], spectra[2 * c + 1], preferred_element_type=F32)
            for c in range(3)
        ]
        motion = [wind[c, span, :].astype(F32) for c in range(3)]
        for c in range(3):
            one, two = (c + 1) % 3, (c + 2) % 3
            emf[c, span, :] = (
                motion[one] * magnetic[two] - motion[two] * magnetic[one]
            ).astype(BF16)
    scale = weights[...]
    for c in range(3):
        for part, table in enumerate((forward_cos, forward_sin)):
            back = jnp.dot(table[...], emf[c], preferred_element_type=F32)
            out[2 * c + part] = (back * scale).astype(BF16)


def grid_product(spectra, first, second, arrange, tables, weights):
    fields, orders, lats = spectra.shape
    whole = lambda array: pl.BlockSpec(array.shape, lambda g: (0,) * array.ndim)
    per_group = pl.BlockSpec((6, orders, lats), lambda g: (g, 0, 0))
    fixed = (first, second, arrange) + tuple(tables) + (weights,)
    return pl.pallas_call(
        grid_kernel,
        grid=(fields // 6,),
        in_specs=[per_group] + [whole(array) for array in fixed],
        out_specs=per_group,
        out_shape=jax.ShapeDtypeStruct(spectra.shape, BF16),
        scratch_shapes=[pltpu.VMEM((3, NLON, lats), BF16)] * 2,
        compiler_params=pltpu.CompilerParams(vmem_limit_bytes=VMEM_CAP),
        cost_estimate=work(16),
        name="grid_product",
    )(spectra, *fixed)


def analysis_kernel(switch, fourier, table, out, *, slots):
    source = pl.program_id(0)
    window = table.shape[1]
    fields = fourier.shape[0]
    pieces = out.shape[2]
    width = out.shape[4]
    sign = mirror_sign(fields)
    lane = lax.broadcasted_iota(jnp.int32, (fields, window), 1)
    blank = jnp.zeros((fields, 128 - (window - NM)), F32)

    def store(values, span):
        for team in range(2):
            for piece in range(pieces):
                row = 2 * (team * pieces + piece)
                out[team, 0, piece, :, span] = values[row : row + 2].astype(BF16)

    def group(index, over):
        rows = pl.ds(pl.multiple_of(index * 2 * SLOTS, 2 * SLOTS), 2 * SLOTS)
        by_order = swap_major(fourier[:, rows, :].astype(F32))
        for slot in range(SLOTS):
            place = index * SLOTS + slot
            in_low, even, _ = row_mask(switch, source, place, slots, lane)
            split = []
            for order in range(2):
                values = by_order[2 * slot + order]
                north, south, rest = values[:, :128], values[:, 128:256], values[:, 256:]
                split += [
                    jnp.concatenate([north + south, rest], axis=1),
                    jnp.concatenate([north - south, rest * sign], axis=1),
                ]
            made = lax.dot_general(
                jnp.concatenate(split, axis=0).astype(BF16),
                table[place],
                (((1,), (1,)), ((), ())),
                preferred_element_type=F32,
            )
            part = [made[k * fields : (k + 1) * fields] for k in range(4)]
            made = jnp.where(
                in_low, jnp.where(even, part[0], part[1]), jnp.where(even, part[2], part[3])
            )
            start = pl.multiple_of(place * NM, NM)
            store(
                jnp.concatenate([made[:, :128] + over, made[:, 128:NM]], axis=1),
                pl.ds(start, NM),
            )
            over = jnp.concatenate([made[:, NM:], blank], axis=1)
        return over

    over = lax.fori_loop(0, slots // SLOTS, group, jnp.zeros((fields, 128), F32))
    full = slots * NM
    store(over[:, : width - full], pl.ds(full, width - full))


def analysis(fourier, table, switch, slots, width):
    fields, orders, lats = fourier.shape
    pairs, window, lanes = table.shape
    sources = pairs // slots
    pieces = fields // 4
    return pl.pallas_call(
        functools.partial(analysis_kernel, slots=slots),
        grid_spec=pltpu.PrefetchScalarGridSpec(
            num_scalar_prefetch=1,
            grid=(sources,),
            in_specs=[
                pl.BlockSpec((fields, 2 * slots, NLAT), lambda z, _: (0, z, 0)),
                pl.BlockSpec((slots, window, lanes), lambda z, _: (z, 0, 0)),
            ],
            out_specs=pl.BlockSpec((2, 1, pieces, 2, width), lambda z, _: (0, z, 0, 0, 0)),
        ),
        out_shape=jax.ShapeDtypeStruct((2, sources, pieces, 2, width), BF16),
        compiler_params=pltpu.CompilerParams(vmem_limit_bytes=VMEM_CAP),
        cost_estimate=work(14),
        name="analysis",
    )(switch, fourier, table)


def pack_kernel(section, out):
    out[0] = section[:, 0, 0]


def pack_level(section, level):
    pieces, targets, _, parts, width = section.shape
    return pl.pallas_call(
        pack_kernel,
        grid=(targets,),
        in_specs=[pl.BlockSpec((pieces, 1, 1, parts, width), lambda d: (0, d, level, 0, 0))],
        out_specs=pl.BlockSpec((1, pieces, parts, width), lambda d: (d, 0, 0, 0)),
        out_shape=jax.ShapeDtypeStruct((targets, pieces, parts, width), BF16),
        cost_estimate=work(5),
        name="pack",
    )(section)


def finish_kernel(base, tendency, out):
    fields = tendency.shape[2]
    for field in range(fields):
        out[0, field, :, :, 0] = base[0, field, :, :, 0] + step_weight * tendency[
            :, :, field
        ].astype(F32)


def finish(total, tendency, level):
    tests, comps, teams, count, depth, parts, width = total.shape
    own = pl.BlockSpec(
        (1, comps, teams, count, 1, parts, width), lambda s: (s, 0, 0, 0, level, 0, 0)
    )
    return pl.pallas_call(
        finish_kernel,
        grid=(tests,),
        in_specs=[
            own,
            pl.BlockSpec((teams, count, comps, parts, width), lambda s: (0, 0, s, 0, 0)),
        ],
        out_specs=own,
        out_shape=jax.ShapeDtypeStruct(total.shape, F32),
        input_output_aliases={0: 0},
        compiler_params=pltpu.CompilerParams(vmem_limit_bytes=VMEM_CAP),
        cost_estimate=work(5),
        name="finish",
    )(total, tendency)


def gather_pairs(pair_list, count):
    own = pair_list.shape[0]
    place = lax.axis_index("ma")
    every = jnp.zeros((count, own), jnp.int32)
    every = lax.dynamic_update_slice(every, pair_list[None], (place, 0))
    for shift in range(1, count):
        moved = lax.ppermute(pair_list, "ma", [(k, (k + shift) % count) for k in range(count)])
        every = lax.dynamic_update_slice(every, moved[None], ((place - shift) % count, 0))
    return every.reshape(-1)


def shards_by_level(section, start, velocity, pair_list, wavenumber, *, count):
    slots = pair_list.shape[0]
    width = section.shape[-1]
    depth = LEV // (2 * count)
    band = velocity.shape[0]
    place = lax.axis_index("ma")
    across = lax.axis_index("x")
    core = lax.axis_index("k")
    swap_cores = [(0, 1), (1, 0)]
    by_level = section.reshape(TESTS * 3, 2 * count, depth, 2, width)
    sent = pack_level(by_level, 0)
    every_pair = gather_pairs(pair_list, count)
    slot_of = jnp.arange(count * slots, dtype=jnp.int32) % slots
    switch = slot_of + NM - every_pair

    other = lax.ppermute(wavenumber, "k", swap_cores)
    waves_here = jnp.where(core == 0, jnp.stack([wavenumber, other]), jnp.stack([other, wavenumber]))
    forcing = jnp.stack([test_field(waves_here[team, 0], TESTS, LEV) for team in range(2)])
    forcing = forcing.reshape(2 * TESTS * 3, LEV)
    forcing = lax.dynamic_slice_in_dim(forcing, (core * count + place) * depth, depth, axis=1)
    forcing = jnp.stack([forcing, jnp.zeros_like(forcing)], axis=1).reshape(-1, depth)

    exchange = functools.partial(
        lax.all_to_all, axis_name=("k", "ma"), split_axis=0, concat_axis=0, tiled=True
    )
    arrived = exchange(sent)
    specs = [arrived]

    side = count // 2
    bands = velocity.transpose(2, 1, 0, 3)
    pieces = []
    for turn in range(side):
        block = lax.dynamic_slice_in_dim(bands, (place + turn) % side * depth, depth, axis=0)
        route = [
            (
                sender * count + origin,
                origin // side * count + sender * side + (origin + turn) % side,
            )
            for sender in range(2)
            for origin in range(count)
        ]
        pieces.append(lax.ppermute(block, ("k", "ma"), route))

    mid = NLAT // 2
    north = jnp.arange(mid, dtype=jnp.int32)
    lats = jnp.concatenate(
        [north[:128], NLAT - 1 - north[:128], north[128:], NLAT - 1 - north[128:]]
    )
    shift = (place - jnp.arange(side, dtype=jnp.int32)) % side
    origin = side * jnp.stack([1 - across, across])[None, :] + shift[:, None]
    rows = band * origin[:, :, None] + jnp.arange(band, dtype=jnp.int32)
    arrange = (rows.reshape(-1)[:, None] == lats[None, :]).astype(BF16)
    half_table, table = legendre_table(every_pair, slots, jnp.concatenate([north, north[128:]]))
    order_list = jnp.stack([every_pair, NM - 1 - every_pair], axis=1).reshape(-1)
    waves = wave_table(order_list, NLON)
    inverse_table = (waves * grid_scale).astype(BF16)
    forward_table = (waves * (2.0 * jnp.pi / NLON)).astype(BF16)
    tables = (inverse_table[0].T, inverse_table[1].T, forward_table[0], forward_table[1])
    weights = lat_weights(lats, NLAT)[None, :]

    row_index = jnp.arange(PAIR_ROWS, dtype=jnp.int32)
    first_half = row_index[None, :] < (NM - pair_list)[:, None]
    degree = jnp.where(first_half, pair_list[:, None] + row_index[None, :], row_index[None, :] - 1)
    spread = (degree * (degree + 1)).astype(F32).reshape(-1)
    total = start[0] - (step_weight * diffusion) * spread * section[0].astype(F32)
    total = total.reshape(TESTS, 3, 2, count, depth, 2, width)

    winds = []
    last = (arrived,)
    for group in (slice(0, 1), slice(1, depth)):
        part = after(jnp.stack([piece[group] for piece in pieces], axis=1), *last)
        turn = lax.ppermute(part, ("x", "k"), [(0, 2), (1, 0), (2, 3), (3, 1)])
        cross = lax.ppermute(part, ("x", "k"), [(1, 2), (2, 1)])
        other = jnp.where(across == core, part, cross)
        winds += [(turn[k], other[k]) for k in range(turn.shape[0])]
        last = (turn, cross)

    first_spectra = synthesis(
        arrived.reshape(2, count, TESTS * 3, 2, width), table, forcing[:, :1], switch, slots
    )
    last = (arrived,)
    for level in range(1, depth):
        packed = pack_level(by_level if level == 1 else after(by_level, arrived), level)
        specs.append(exchange(after(packed, *last)))
        last = (specs[-1],)
    specs = [spec.reshape(2, count, TESTS * 3, 2, width) for spec in specs]

    for level in range(depth):
        spectra = first_spectra
        if level:
            spectra = synthesis(specs[level], table, forcing[:, level : level + 1], switch, slots)
        fourier = grid_product(spectra, *winds[level], arrange, tables, weights)
        tendency = analysis(fourier, table, switch, slots, width)
        back = exchange(after(tendency.reshape(2 * count, TESTS * 3, 2, width), *last))
        last = (back,)
        total = finish(total, back.reshape(2, count, TESTS * 3, 2, width), level)
    return total.reshape(start.shape)


def solution(mesh):
    sizes = dict(mesh.shape)
    count = sizes["ma"]
    whole_slots = (NM // 2) % (count * SLOTS) == 0
    if sizes["team"] == 4 and count % 2 == 0 and LEV % (2 * count) == 0 and whole_slots:
        grid = Mesh(
            mesh.devices.reshape(sizes["run"], 2, 2, count), ("run", "x", "k", "ma")
        )
        team = ("x", "k")
        body = lambda *arrays: shards_by_level(*arrays, count=count)
    else:
        grid, team, body = mesh, ("team",), shards_general
    placed = (
        P(("run",) + team, None, None, None, None, "ma"),
        P(("run",) + team, None, None, None, None, "ma"),
        P(("run", "ma"), None, team, None),
        P("ma"),
        P(team),
    )
    return jax.shard_map(
        body,
        mesh=grid,
        in_specs=placed,
        out_specs=P(("run",) + team, None, None, None, None, "ma"),
        check_vma=False,
    )
```

```python
import functools
import math

import jax
import jax.numpy as jnp
from jax import lax
from jax.experimental import pallas as pl
from jax.experimental.pallas import tpu as pltpu
from jax.sharding import Mesh, PartitionSpec as P

NM = 256
NLAT = 384
NLON = 768
LEV = 24
TESTS = 2


grid_scale = 1.0 / 64.0
anchor_gain = 64.0 * math.sqrt(4.0 * math.pi)
quadrature_gain = 64.0
diffusion = 7e-06
step_weight = 2.0
row_block = 16


def seed_values(order_real, order_count, sine_theta):
    factor_index = jnp.arange(1, order_count, dtype=jnp.float32)
    factor_log = jnp.log((2.0 * factor_index - 1.0) / (2.0 * factor_index))
    partial_log = jnp.sum(
        jnp.where(factor_index[None, :] <= order_real[:, None], factor_log[None, :], 0.0), axis=1
    )
    seed_log = 0.5 * (jnp.log((2.0 * order_real + 1.0) / (4.0 * jnp.pi)) + partial_log)
    return jnp.exp(seed_log[:, None] + order_real[:, None] * jnp.log(sine_theta)[None, :])


def pair_table(pair_ids, order_count, lat_count):
    pair_count = pair_ids.shape[0]
    order_low = pair_ids.astype(jnp.float32)
    order_high = (order_count - 1 - pair_ids).astype(jnp.float32)
    colatitude = jnp.pi * (jnp.arange(lat_count, dtype=jnp.float32) + 0.5) / lat_count
    cosine = jnp.cos(colatitude)
    sine_theta = jnp.sin(colatitude)
    seed_low = seed_values(order_low, order_count, sine_theta)
    seed_high = seed_values(order_high, order_count, sine_theta)
    switch_row = order_count - pair_ids

    def one_row(state_pair, row_id):
        latest, before = state_pair
        in_low = row_id < switch_row
        degree = jnp.where(in_low, pair_ids + row_id, row_id - 1)
        order_real = jnp.where(in_low, order_low, order_high)
        degree_real = degree.astype(jnp.float32)
        active = degree_real > order_real
        divisor = jnp.where(active, degree_real * degree_real - order_real * order_real, 1.0)
        upper = jnp.sqrt(jnp.maximum(4.0 * degree_real * degree_real - 1.0, 0.0) / divisor)
        lower_num = ((degree_real - 1.0) * (degree_real - 1.0) - order_real * order_real) * (
            2.0 * degree_real + 1.0
        )
        lower = jnp.sqrt(
            jnp.maximum(lower_num, 0.0) / (divisor * jnp.maximum(2.0 * degree_real - 3.0, 1.0))
        )
        recurred = upper[:, None] * cosine[None, :] * latest - lower[:, None] * before
        is_seed = (row_id == 0) | (row_id == switch_row)
        seeded = jnp.where(in_low[:, None], seed_low, seed_high)
        current = jnp.where(is_seed[:, None], seeded, jnp.where(active[:, None], recurred, 0.0))
        return ((current, latest), current)

    def block_rows(state_pair, first_row):
        produced = []
        for offset in range(row_block):
            state_pair, current = one_row(state_pair, first_row + offset)
            produced.append(current)
        return (state_pair, jnp.stack(produced))

    turns = -(-(order_count + 1) // row_block)
    blank_rows = jnp.zeros((pair_count, lat_count), jnp.float32)
    firsts = jnp.arange(turns, dtype=jnp.int32) * row_block
    _, values = lax.scan(block_rows, (blank_rows, blank_rows), firsts)
    leg_table = values.reshape(turns * row_block, pair_count, lat_count)[: order_count + 1]
    row_index = jnp.arange(order_count + 1, dtype=jnp.int32)
    first_half = row_index[None, :] < (order_count - pair_ids)[:, None]
    degree = jnp.where(first_half, pair_ids[:, None] + row_index[None, :], row_index[None, :] - 1)
    return (leg_table, first_half, degree)


def wave_table(order_list, lon_count):
    longitude = jnp.arange(lon_count, dtype=jnp.int32)
    phase_index = order_list[:, None] * longitude[None, :] % lon_count
    angle_rad = 2.0 * jnp.pi / lon_count * phase_index.astype(jnp.float32)
    return jnp.stack([jnp.cos(angle_rad), jnp.sin(angle_rad)])


def lat_weights(latitudes, lat_count):
    colatitude = jnp.pi * (latitudes.astype(jnp.float32) + 0.5) / lat_count
    return quadrature_gain * (jnp.pi / lat_count) * jnp.sin(colatitude)


def test_field(wave_index, test_count, levels):
    component = jnp.arange(3, dtype=jnp.int32)
    test_ids = jnp.arange(test_count, dtype=jnp.int32)
    level_ids = jnp.arange(levels, dtype=jnp.float32)
    aligned = (component[None, :] == test_ids[:, None]).astype(jnp.float32)
    profile = jnp.cos(jnp.pi * wave_index.astype(jnp.float32) * (level_ids + 0.5) / levels)
    return anchor_gain * aligned[:, :, None] * profile[None, None, :]


def cross_field(motion, magnetic, along):
    return jnp.roll(motion, -1, along) * jnp.roll(magnetic, -2, along) - jnp.roll(
        motion, -2, along
    ) * jnp.roll(magnetic, -1, along)


def shards_general(section, start, velocity, pair_list, wavenumber):
    pair_count = pair_list.shape[0]
    leg_table, first_half, degree = pair_table(pair_list, NM, NLAT)
    legendre = leg_table.astype(jnp.bfloat16)
    selectors = jnp.stack([first_half, jnp.logical_not(first_half)], axis=1)
    masks_low = selectors.astype(jnp.bfloat16)
    anchor = (pair_list == 0)[:, None] & (jnp.arange(NM + 1) == 0)[None, :]
    anchor_rows = anchor.reshape(-1).astype(jnp.float32)
    part_pick = jnp.array([1.0, 0.0], jnp.float32)
    forcing = test_field(wavenumber[0], TESTS, LEV)
    spec_field = (
        section[0].astype(jnp.float32)
        + forcing[:, :, :, None, None] * part_pick[:, None] * anchor_rows[None, :]
    )
    spec_field = spec_field.astype(jnp.bfloat16).reshape(TESTS, 3, LEV, 2, pair_count, NM + 1)
    masked = spec_field[:, :, :, :, :, None, :] * masks_low
    spectra = jnp.einsum(
        "scvpqhr,rqa->ascvpqh", masked, legendre, preferred_element_type=jnp.float32
    )
    spectra = spectra.astype(jnp.bfloat16).reshape(NLAT, TESTS, 3, LEV, 2, 2 * pair_count)
    every_pair = lax.all_gather(pair_list, "ma", axis=0, tiled=True)
    order_list = jnp.stack([every_pair, NM - 1 - every_pair], axis=1).reshape(-1)
    waves = wave_table(order_list, NLON)
    inverse_table = (waves * grid_scale).astype(jnp.bfloat16)
    forward_table = (waves * (2.0 * jnp.pi / NLON)).astype(jnp.bfloat16)
    wind_field = lax.all_gather(velocity, "team", axis=2, tiled=True)
    band_size = velocity.shape[0]
    latitudes = lax.axis_index("ma") * band_size + jnp.arange(band_size, dtype=jnp.int32)
    weights = lat_weights(latitudes, NLAT)
    collected = []
    for test_id in range(TESTS):
        grid_field = jnp.einsum(
            "ascvpm,pmo->ascvo",
            lax.all_to_all(
                spectra[:, test_id : test_id + 1], "ma", split_axis=0, concat_axis=5, tiled=True
            ),
            inverse_table,
            preferred_element_type=jnp.float32,
        )
        emf = cross_field(wind_field[:, None], grid_field, 2).astype(jnp.bfloat16)
        fourier = jnp.einsum(
            "ascvo,pmo->ascvpm", emf, forward_table, preferred_element_type=jnp.float32
        )
        fourier = (fourier * weights[:, None, None, None, None, None]).astype(jnp.bfloat16)
        collected.append(lax.all_to_all(fourier, "ma", split_axis=5, concat_axis=0, tiled=True))
    returned = jnp.concatenate(collected, axis=1)
    returned = returned.reshape(NLAT, TESTS, 3, LEV, 2, pair_count, 2)
    project = jnp.einsum(
        "ascvpqh,rqa->scvpqhr", returned, legendre, preferred_element_type=jnp.float32
    )
    tendency = jnp.sum(project * selectors.astype(jnp.float32), axis=5).reshape(
        TESTS, 3, LEV, 2, -1
    )
    spread = (degree * (degree + 1)).astype(jnp.float32).reshape(-1)
    updated = start[0] + step_weight * (
        tendency - diffusion * spread * section[0].astype(jnp.float32)
    )
    return updated[None]


BF16 = jnp.bfloat16
F32 = jnp.float32
VMEM_CAP = 56 << 20
PAIR_ROWS = NM + 1
CHUNK_ROWS = 16
TABLE_PAIRS = 16
SLOTS = 16


def work(micros):
    return pl.CostEstimate(
        flops=int(micros * 1e9), transcendentals=0, bytes_accessed=int(micros * 1e6)
    )


def after(value, *others):
    return lax.optimization_barrier((value,) + others)[0]


def table_window(slots):
    return -(-(PAIR_ROWS + slots - 1) // 32) * 32


def swap_major(block):
    return jnp.swapaxes(block, 0, 1)


def table_kernel(upper, lower, first, second, seed_low, seed_high, cosine, _, out, *, lead):
    shape = seed_low.shape
    cosine_rows = jnp.broadcast_to(cosine[...], shape)
    first_step = first[...]
    second_step = second[...]
    low_value = seed_low[...]
    high_value = seed_high[...]

    def chunk(starting, index, state):
        latest, before = state
        scale_up = upper[index]
        scale_down = lower[index]
        produced = []
        for offset in range(CHUNK_ROWS):
            step = index * CHUNK_ROWS + offset
            current = (scale_up[:, offset : offset + 1] * cosine_rows) * latest - scale_down[
                :, offset : offset + 1
            ] * before
            current = jnp.where(second_step == step, high_value, current)
            if starting:
                current = jnp.where(first_step == step, low_value, current)
            produced.append(current)
            latest, before = current, latest
        rows = swap_major(jnp.stack(produced))
        out[:, pl.ds(pl.multiple_of(index * CHUNK_ROWS, CHUNK_ROWS), CHUNK_ROWS), :] = rows.astype(
            BF16
        )
        return latest, before

    blank = jnp.zeros(shape, F32)
    state = lax.fori_loop(0, lead, functools.partial(chunk, True), (blank, blank))
    lax.fori_loop(lead, out.shape[1] // CHUNK_ROWS, functools.partial(chunk, False), state)


def legendre_table(every_pair, slots, lats):
    pairs = every_pair.shape[0]
    window = table_window(slots)
    order_low = every_pair.astype(F32)
    order_high = (NM - 1 - every_pair).astype(F32)
    colatitude = jnp.pi * (lats.astype(F32) + 0.5) / NLAT
    seed_low = seed_values(order_low, NM, jnp.sin(colatitude))
    seed_high = seed_values(order_high, NM, jnp.sin(colatitude))
    slot = jnp.arange(pairs, dtype=jnp.int32) % slots
    row = jnp.arange(window, dtype=jnp.int32)[None, :] - slot[:, None]
    switch = NM - every_pair
    in_low = row < switch[:, None]
    degree = jnp.where(in_low, every_pair[:, None] + row, row - 1)
    order = jnp.where(in_low, order_low[:, None], order_high[:, None])
    real = degree.astype(F32)
    active = (real > order) & (row >= 0) & (row < PAIR_ROWS)
    divisor = jnp.where(active, real * real - order * order, 1.0)
    upper = jnp.sqrt(jnp.maximum(4.0 * real * real - 1.0, 0.0) / divisor)
    lower_num = ((real - 1.0) * (real - 1.0) - order * order) * (2.0 * real + 1.0)
    lower = jnp.sqrt(
        jnp.maximum(lower_num, 0.0) / (divisor * jnp.maximum(2.0 * real - 3.0, 1.0))
    )
    by_chunk = lambda values: jnp.swapaxes(
        jnp.where(active, values, 0.0).reshape(pairs, window // CHUNK_ROWS, CHUNK_ROWS), 0, 1
    )
    lanes = lats.shape[0]
    spread_out = lambda values: jnp.broadcast_to(values[:, None], (pairs, lanes))
    chunks = window // CHUNK_ROWS
    operands = (
        by_chunk(upper),
        by_chunk(lower),
        spread_out(slot),
        spread_out(slot + switch),
        seed_low,
        seed_high,
        jnp.cos(colatitude)[None, :],
    )
    blocks = pairs // TABLE_PAIRS
    shape = jax.ShapeDtypeStruct((pairs, window, lanes), BF16)
    halves = []
    for begin, end in ((0, blocks // 2), (blocks // 2, blocks)):
        place = lambda q, begin=begin: q + begin
        coefficient = pl.BlockSpec(
            (chunks, TABLE_PAIRS, CHUNK_ROWS), lambda q, place=place: (0, place(q), 0)
        )
        per_pair = pl.BlockSpec((TABLE_PAIRS, lanes), lambda q, place=place: (place(q), 0))
        before = halves[-1:] or [jnp.zeros((8, 128), BF16)]
        halves.append(
            pl.pallas_call(
                functools.partial(table_kernel, lead=-(-slots // CHUNK_ROWS)),
                grid=(end - begin,),
                in_specs=[coefficient, coefficient, per_pair, per_pair, per_pair, per_pair]
                + [pl.BlockSpec((1, lanes), lambda q: (0, 0))]
                + [pl.BlockSpec(memory_space=pl.ANY)],
                out_specs=pl.BlockSpec(
                    (TABLE_PAIRS, window, lanes), lambda q, place=place: (place(q), 0, 0)
                ),
                out_shape=shape,
                input_output_aliases={7: 0} if halves else {},
                compiler_params=pltpu.CompilerParams(vmem_limit_bytes=VMEM_CAP),
                cost_estimate=work(20),
                name="table",
            )(*operands, *before)
        )
    return halves


def row_mask(switch, source, place, slots, lane):
    turn = switch[source * slots + place]
    in_low = lane < turn
    even = ((lane - jnp.where(in_low, place, turn)) & 1) == 0
    anchor = (lane == place) & (turn == place + NM)
    return in_low, even, anchor


def mirror_sign(fields):
    lane = lax.broadcasted_iota(jnp.int32, (fields, 128), 1)
    return jnp.where(lane < 64, 1.0, -1.0).astype(F32)


def synthesis_kernel(switch, spec, table, forcing, out, *, slots):
    source = pl.program_id(0)
    window = table.shape[1]
    pieces = spec.shape[2]
    fields = 4 * pieces
    sign = mirror_sign(fields)
    lane = lax.broadcasted_iota(jnp.int32, (fields, window), 1)
    force = jnp.broadcast_to(forcing[...], (fields, window))

    def group(index, _):
        collected = []
        for slot in range(SLOTS):
            place = index * SLOTS + slot
            in_low, even, anchor = row_mask(switch, source, place, slots, lane)
            span = pl.ds(pl.multiple_of(place * NM, NM), window)
            rows = jnp.concatenate(
                [
                    spec[team, 0, piece, :, span].astype(F32)
                    for team in range(2)
                    for piece in range(pieces)
                ],
                axis=0,
            )
            rows = rows + jnp.where(anchor, force, 0.0)
            low, high = jnp.where(in_low, rows, 0.0), jnp.where(in_low, 0.0, rows)
            split = [
                jnp.where(even, low, 0.0),
                jnp.where(even, 0.0, low),
                jnp.where(even, high, 0.0),
                jnp.where(even, 0.0, high),
            ]
            made = jnp.dot(
                jnp.concatenate(split, axis=0).astype(BF16),
                table[place],
                preferred_element_type=F32,
            )
            for order in range(2):
                same = made[2 * order * fields : (2 * order + 1) * fields]
                flips = made[(2 * order + 1) * fields : (2 * order + 2) * fields]
                collected.append(
                    jnp.concatenate(
                        [
                            same[:, :128] + flips[:, :128],
                            same[:, :128] - flips[:, :128],
                            same[:, 128:] + sign * flips[:, 128:],
                        ],
                        axis=1,
                    )
                )
        rows = pl.ds(pl.multiple_of(index * 2 * SLOTS, 2 * SLOTS), 2 * SLOTS)
        out[:, rows, :] = swap_major(jnp.stack(collected)).astype(BF16)
        return 0

    lax.fori_loop(0, slots // SLOTS, group, 0)


def synthesis(spec, table, forcing, switch, slots):
    _, sources, pieces, parts, width = spec.shape
    fields = 2 * pieces * parts
    pairs, window, lanes = table.shape
    return pl.pallas_call(
        functools.partial(synthesis_kernel, slots=slots),
        grid_spec=pltpu.PrefetchScalarGridSpec(
            num_scalar_prefetch=1,
            grid=(sources,),
            in_specs=[
                pl.BlockSpec((2, 1, pieces, parts, width), lambda z, _: (0, z, 0, 0, 0)),
                pl.BlockSpec((slots, window, lanes), lambda z, _: (z, 0, 0)),
                pl.BlockSpec((fields, 1), lambda z, _: (0, 0)),
            ],
            out_specs=pl.BlockSpec((fields, 2 * slots, NLAT), lambda z, _: (0, z, 0)),
        ),
        out_shape=jax.ShapeDtypeStruct((fields, 2 * pairs, NLAT), BF16),
        compiler_params=pltpu.CompilerParams(vmem_limit_bytes=VMEM_CAP),
        cost_estimate=work(14),
        name="synthesis",
    )(switch, spec, table, forcing)


LON_TILE = 768


def grid_kernel(
    spectra, first, second, arrange, inverse_cos, inverse_sin, forward_cos, forward_sin, weights,
    out, wind, emf,
):
    @pl.when(pl.program_id(0) == 0)
    def _():
        for c in range(3):
            bands = [
                half[z, c] for z in range(first.shape[0]) for half in (first, second)
            ]
            wind[c] = lax.dot_general(
                jnp.concatenate(bands, axis=0),
                arrange[...],
                (((0,), (0,)), ((), ())),
                preferred_element_type=F32,
            ).astype(BF16)

    for tile in range(NLON // LON_TILE):
        span = pl.ds(tile * LON_TILE, LON_TILE)
        magnetic = [
            jnp.dot(inverse_cos[span, :], spectra[2 * c], preferred_element_type=F32)
            + jnp.dot(inverse_sin[span, :], spectra[2 * c + 1], preferred_element_type=F32)
            for c in range(3)
        ]
        motion = [wind[c, span, :].astype(F32) for c in range(3)]
        for c in range(3):
            one, two = (c + 1) % 3, (c + 2) % 3
            emf[c, span, :] = (
                motion[one] * magnetic[two] - motion[two] * magnetic[one]
            ).astype(BF16)
    scale = weights[...]
    for c in range(3):
        for part, table in enumerate((forward_cos, forward_sin)):
            back = jnp.dot(table[...], emf[c], preferred_element_type=F32)
            out[2 * c + part] = (back * scale).astype(BF16)


def grid_product(spectra, first, second, arrange, tables, weights):
    fields, orders, lats = spectra.shape
    whole = lambda array: pl.BlockSpec(array.shape, lambda g: (0,) * array.ndim)
    per_group = pl.BlockSpec((6, orders, lats), lambda g: (g, 0, 0))
    fixed = (first, second, arrange) + tuple(tables) + (weights,)
    return pl.pallas_call(
        grid_kernel,
        grid=(fields // 6,),
        in_specs=[per_group] + [whole(array) for array in fixed],
        out_specs=per_group,
        out_shape=jax.ShapeDtypeStruct(spectra.shape, BF16),
        scratch_shapes=[pltpu.VMEM((3, NLON, lats), BF16)] * 2,
        compiler_params=pltpu.CompilerParams(vmem_limit_bytes=VMEM_CAP),
        cost_estimate=work(16),
        name="grid_product",
    )(spectra, *fixed)


def analysis_kernel(switch, fourier, table, out, *, slots):
    source = pl.program_id(0)
    window = table.shape[1]
    fields = fourier.shape[0]
    pieces = out.shape[2]
    width = out.shape[4]
    sign = mirror_sign(fields)
    lane = lax.broadcasted_iota(jnp.int32, (fields, window), 1)
    blank = jnp.zeros((fields, 128 - (window - NM)), F32)

    def store(values, span):
        for team in range(2):
            for piece in range(pieces):
                row = 2 * (team * pieces + piece)
                out[team, 0, piece, :, span] = values[row : row + 2].astype(BF16)

    def group(index, over):
        rows = pl.ds(pl.multiple_of(index * 2 * SLOTS, 2 * SLOTS), 2 * SLOTS)
        by_order = swap_major(fourier[:, rows, :].astype(F32))
        for slot in range(SLOTS):
            place = index * SLOTS + slot
            in_low, even, _ = row_mask(switch, source, place, slots, lane)
            split = []
            for order in range(2):
                values = by_order[2 * slot + order]
                north, south, rest = values[:, :128], values[:, 128:256], values[:, 256:]
                split += [
                    jnp.concatenate([north + south, rest], axis=1),
                    jnp.concatenate([north - south, rest * sign], axis=1),
                ]
            made = lax.dot_general(
                jnp.concatenate(split, axis=0).astype(BF16),
                table[place],
                (((1,), (1,)), ((), ())),
                preferred_element_type=F32,
            )
            part = [made[k * fields : (k + 1) * fields] for k in range(4)]
            made = jnp.where(
                in_low, jnp.where(even, part[0], part[1]), jnp.where(even, part[2], part[3])
            )
            start = pl.multiple_of(place * NM, NM)
            store(
                jnp.concatenate([made[:, :128] + over, made[:, 128:NM]], axis=1),
                pl.ds(start, NM),
            )
            over = jnp.concatenate([made[:, NM:], blank], axis=1)
        return over

    over = lax.fori_loop(0, slots // SLOTS, group, jnp.zeros((fields, 128), F32))
    full = slots * NM
    store(over[:, : width - full], pl.ds(full, width - full))


def analysis(fourier, table, switch, slots, width):
    fields, orders, lats = fourier.shape
    pairs, window, lanes = table.shape
    sources = pairs // slots
    pieces = fields // 4
    return pl.pallas_call(
        functools.partial(analysis_kernel, slots=slots),
        grid_spec=pltpu.PrefetchScalarGridSpec(
            num_scalar_prefetch=1,
            grid=(sources,),
            in_specs=[
                pl.BlockSpec((fields, 2 * slots, NLAT), lambda z, _: (0, z, 0)),
                pl.BlockSpec((slots, window, lanes), lambda z, _: (z, 0, 0)),
            ],
            out_specs=pl.BlockSpec((2, 1, pieces, 2, width), lambda z, _: (0, z, 0, 0, 0)),
        ),
        out_shape=jax.ShapeDtypeStruct((2, sources, pieces, 2, width), BF16),
        compiler_params=pltpu.CompilerParams(vmem_limit_bytes=VMEM_CAP),
        cost_estimate=work(14),
        name="analysis",
    )(switch, fourier, table)


def pack_kernel(section, out):
    out[0] = section[:, 0, 0]


def pack_level(section, level):
    pieces, targets, _, parts, width = section.shape
    return pl.pallas_call(
        pack_kernel,
        grid=(targets,),
        in_specs=[pl.BlockSpec((pieces, 1, 1, parts, width), lambda d: (0, d, level, 0, 0))],
        out_specs=pl.BlockSpec((1, pieces, parts, width), lambda d: (d, 0, 0, 0)),
        out_shape=jax.ShapeDtypeStruct((targets, pieces, parts, width), BF16),
        cost_estimate=work(5),
        name="pack",
    )(section)


def finish_kernel(base, tendency, out):
    fields = tendency.shape[2]
    for field in range(fields):
        out[0, field, :, :, 0] = base[0, field, :, :, 0] + step_weight * tendency[
            :, :, field
        ].astype(F32)


def finish(total, tendency, level):
    tests, comps, teams, count, depth, parts, width = total.shape
    own = pl.BlockSpec(
        (1, comps, teams, count, 1, parts, width), lambda s: (s, 0, 0, 0, level, 0, 0)
    )
    return pl.pallas_call(
        finish_kernel,
        grid=(tests,),
        in_specs=[
            own,
            pl.BlockSpec((teams, count, comps, parts, width), lambda s: (0, 0, s, 0, 0)),
        ],
        out_specs=own,
        out_shape=jax.ShapeDtypeStruct(total.shape, F32),
        input_output_aliases={0: 0},
        compiler_params=pltpu.CompilerParams(vmem_limit_bytes=VMEM_CAP),
        cost_estimate=work(5),
        name="finish",
    )(total, tendency)


def gather_pairs(pair_list, count):
    own = pair_list.shape[0]
    place = lax.axis_index("ma")
    every = jnp.zeros((count, own), jnp.int32)
    every = lax.dynamic_update_slice(every, pair_list[None], (place, 0))
    for shift in range(1, count):
        moved = lax.ppermute(pair_list, "ma", [(k, (k + shift) % count) for k in range(count)])
        every = lax.dynamic_update_slice(every, moved[None], ((place - shift) % count, 0))
    return every.reshape(-1)


def shards_by_level(section, start, velocity, pair_list, wavenumber, *, count):
    slots = pair_list.shape[0]
    width = section.shape[-1]
    depth = LEV // (2 * count)
    band = velocity.shape[0]
    place = lax.axis_index("ma")
    across = lax.axis_index("x")
    core = lax.axis_index("k")
    swap_cores = [(0, 1), (1, 0)]
    by_level = section.reshape(TESTS * 3, 2 * count, depth, 2, width)
    sent = pack_level(by_level, 0)
    every_pair = gather_pairs(pair_list, count)
    slot_of = jnp.arange(count * slots, dtype=jnp.int32) % slots
    switch = slot_of + NM - every_pair

    other = lax.ppermute(wavenumber, "k", swap_cores)
    waves_here = jnp.where(core == 0, jnp.stack([wavenumber, other]), jnp.stack([other, wavenumber]))
    forcing = jnp.stack([test_field(waves_here[team, 0], TESTS, LEV) for team in range(2)])
    forcing = forcing.reshape(2 * TESTS * 3, LEV)
    forcing = lax.dynamic_slice_in_dim(forcing, (core * count + place) * depth, depth, axis=1)
    forcing = jnp.stack([forcing, jnp.zeros_like(forcing)], axis=1).reshape(-1, depth)

    exchange = functools.partial(
        lax.all_to_all, axis_name=("k", "ma"), split_axis=0, concat_axis=0, tiled=True
    )
    arrived = exchange(sent)
    specs = [arrived]

    side = count // 2
    bands = velocity.transpose(2, 1, 0, 3)
    pieces = []
    for turn in range(side):
        block = lax.dynamic_slice_in_dim(bands, (place + turn) % side * depth, depth, axis=0)
        route = [
            (
                sender * count + origin,
                origin // side * count + sender * side + (origin + turn) % side,
            )
            for sender in range(2)
            for origin in range(count)
        ]
        pieces.append(lax.ppermute(block, ("k", "ma"), route))

    mid = NLAT // 2
    north = jnp.arange(mid, dtype=jnp.int32)
    lats = jnp.concatenate(
        [north[:128], NLAT - 1 - north[:128], north[128:], NLAT - 1 - north[128:]]
    )
    shift = (place - jnp.arange(side, dtype=jnp.int32)) % side
    origin = side * jnp.stack([1 - across, across])[None, :] + shift[:, None]
    rows = band * origin[:, :, None] + jnp.arange(band, dtype=jnp.int32)
    arrange = (rows.reshape(-1)[:, None] == lats[None, :]).astype(BF16)
    half_table, table = legendre_table(every_pair, slots, jnp.concatenate([north, north[128:]]))
    order_list = jnp.stack([every_pair, NM - 1 - every_pair], axis=1).reshape(-1)
    waves = wave_table(order_list, NLON)
    inverse_table = (waves * grid_scale).astype(BF16)
    forward_table = (waves * (2.0 * jnp.pi / NLON)).astype(BF16)
    tables = (inverse_table[0].T, inverse_table[1].T, forward_table[0], forward_table[1])
    weights = lat_weights(lats, NLAT)[None, :]

    row_index = jnp.arange(PAIR_ROWS, dtype=jnp.int32)
    first_half = row_index[None, :] < (NM - pair_list)[:, None]
    degree = jnp.where(first_half, pair_list[:, None] + row_index[None, :], row_index[None, :] - 1)
    spread = (degree * (degree + 1)).astype(F32).reshape(-1)
    total = start[0] - (step_weight * diffusion) * spread * section[0].astype(F32)
    total = total.reshape(TESTS, 3, 2, count, depth, 2, width)

    winds = []
    last = (arrived,)
    for group in (slice(0, 1), slice(1, depth)):
        part = after(jnp.stack([piece[group] for piece in pieces], axis=1), *last)
        turn = lax.ppermute(part, ("x", "k"), [(0, 2), (1, 0), (2, 3), (3, 1)])
        cross = lax.ppermute(part, ("x", "k"), [(1, 2), (2, 1)])
        other = jnp.where(across == core, part, cross)
        winds += [(turn[k], other[k]) for k in range(turn.shape[0])]
        last = (turn, cross)

    first_spectra = synthesis(
        arrived.reshape(2, count, TESTS * 3, 2, width), table, forcing[:, :1], switch, slots
    )
    last = (arrived,)
    for level in range(1, depth):
        packed = pack_level(by_level, level)
        specs.append(exchange(after(packed, *last)))
        last = (specs[-1],)
    specs = [spec.reshape(2, count, TESTS * 3, 2, width) for spec in specs]

    for level in range(depth):
        spectra = first_spectra
        if level:
            spectra = synthesis(specs[level], table, forcing[:, level : level + 1], switch, slots)
        fourier = grid_product(spectra, *winds[level], arrange, tables, weights)
        tendency = analysis(fourier, table, switch, slots, width)
        back = exchange(after(tendency.reshape(2 * count, TESTS * 3, 2, width), *last))
        last = (back,)
        total = finish(total, back.reshape(2, count, TESTS * 3, 2, width), level)
    return total.reshape(start.shape)


def solution(mesh):
    sizes = dict(mesh.shape)
    count = sizes["ma"]
    whole_slots = (NM // 2) % (count * SLOTS) == 0
    if sizes["team"] == 4 and count % 2 == 0 and LEV % (2 * count) == 0 and whole_slots:
        grid = Mesh(
            mesh.devices.reshape(sizes["run"], 2, 2, count), ("run", "x", "k", "ma")
        )
        team = ("x", "k")
        body = lambda *arrays: shards_by_level(*arrays, count=count)
    else:
        grid, team, body = mesh, ("team",), shards_general
    placed = (
        P(("run",) + team, None, None, None, None, "ma"),
        P(("run",) + team, None, None, None, None, "ma"),
        P(("run", "ma"), None, team, None),
        P("ma"),
        P(team),
    )
    return jax.shard_map(
        body,
        mesh=grid,
        in_specs=placed,
        out_specs=P(("run",) + team, None, None, None, None, "ma"),
        check_vma=False,
    )
```

```python
import functools
import math

import jax
import jax.numpy as jnp
from jax import lax
from jax.experimental import pallas as pl
from jax.experimental.pallas import tpu as pltpu
from jax.sharding import Mesh, PartitionSpec as P

NM = 256
NLAT = 384
NLON = 768
LEV = 24
TESTS = 2


grid_scale = 1.0 / 64.0
anchor_gain = 64.0 * math.sqrt(4.0 * math.pi)
quadrature_gain = 64.0
diffusion = 7e-06
step_weight = 2.0
row_block = 16


def seed_values(order_real, order_count, sine_theta):
    factor_index = jnp.arange(1, order_count, dtype=jnp.float32)
    factor_log = jnp.log((2.0 * factor_index - 1.0) / (2.0 * factor_index))
    partial_log = jnp.sum(
        jnp.where(factor_index[None, :] <= order_real[:, None], factor_log[None, :], 0.0), axis=1
    )
    seed_log = 0.5 * (jnp.log((2.0 * order_real + 1.0) / (4.0 * jnp.pi)) + partial_log)
    return jnp.exp(seed_log[:, None] + order_real[:, None] * jnp.log(sine_theta)[None, :])


def pair_table(pair_ids, order_count, lat_count):
    pair_count = pair_ids.shape[0]
    order_low = pair_ids.astype(jnp.float32)
    order_high = (order_count - 1 - pair_ids).astype(jnp.float32)
    colatitude = jnp.pi * (jnp.arange(lat_count, dtype=jnp.float32) + 0.5) / lat_count
    cosine = jnp.cos(colatitude)
    sine_theta = jnp.sin(colatitude)
    seed_low = seed_values(order_low, order_count, sine_theta)
    seed_high = seed_values(order_high, order_count, sine_theta)
    switch_row = order_count - pair_ids

    def one_row(state_pair, row_id):
        latest, before = state_pair
        in_low = row_id < switch_row
        degree = jnp.where(in_low, pair_ids + row_id, row_id - 1)
        order_real = jnp.where(in_low, order_low, order_high)
        degree_real = degree.astype(jnp.float32)
        active = degree_real > order_real
        divisor = jnp.where(active, degree_real * degree_real - order_real * order_real, 1.0)
        upper = jnp.sqrt(jnp.maximum(4.0 * degree_real * degree_real - 1.0, 0.0) / divisor)
        lower_num = ((degree_real - 1.0) * (degree_real - 1.0) - order_real * order_real) * (
            2.0 * degree_real + 1.0
        )
        lower = jnp.sqrt(
            jnp.maximum(lower_num, 0.0) / (divisor * jnp.maximum(2.0 * degree_real - 3.0, 1.0))
        )
        recurred = upper[:, None] * cosine[None, :] * latest - lower[:, None] * before
        is_seed = (row_id == 0) | (row_id == switch_row)
        seeded = jnp.where(in_low[:, None], seed_low, seed_high)
        current = jnp.where(is_seed[:, None], seeded, jnp.where(active[:, None], recurred, 0.0))
        return ((current, latest), current)

    def block_rows(state_pair, first_row):
        produced = []
        for offset in range(row_block):
            state_pair, current = one_row(state_pair, first_row + offset)
            produced.append(current)
        return (state_pair, jnp.stack(produced))

    turns = -(-(order_count + 1) // row_block)
    blank_rows = jnp.zeros((pair_count, lat_count), jnp.float32)
    firsts = jnp.arange(turns, dtype=jnp.int32) * row_block
    _, values = lax.scan(block_rows, (blank_rows, blank_rows), firsts)
    leg_table = values.reshape(turns * row_block, pair_count, lat_count)[: order_count + 1]
    row_index = jnp.arange(order_count + 1, dtype=jnp.int32)
    first_half = row_index[None, :] < (order_count - pair_ids)[:, None]
    degree = jnp.where(first_half, pair_ids[:, None] + row_index[None, :], row_index[None, :] - 1)
    return (leg_table, first_half, degree)


def wave_table(order_list, lon_count):
    longitude = jnp.arange(lon_count, dtype=jnp.int32)
    phase_index = order_list[:, None] * longitude[None, :] % lon_count
    angle_rad = 2.0 * jnp.pi / lon_count * phase_index.astype(jnp.float32)
    return jnp.stack([jnp.cos(angle_rad), jnp.sin(angle_rad)])


def lat_weights(latitudes, lat_count):
    colatitude = jnp.pi * (latitudes.astype(jnp.float32) + 0.5) / lat_count
    return quadrature_gain * (jnp.pi / lat_count) * jnp.sin(colatitude)


def test_field(wave_index, test_count, levels):
    component = jnp.arange(3, dtype=jnp.int32)
    test_ids = jnp.arange(test_count, dtype=jnp.int32)
    level_ids = jnp.arange(levels, dtype=jnp.float32)
    aligned = (component[None, :] == test_ids[:, None]).astype(jnp.float32)
    profile = jnp.cos(jnp.pi * wave_index.astype(jnp.float32) * (level_ids + 0.5) / levels)
    return anchor_gain * aligned[:, :, None] * profile[None, None, :]


def cross_field(motion, magnetic, along):
    return jnp.roll(motion, -1, along) * jnp.roll(magnetic, -2, along) - jnp.roll(
        motion, -2, along
    ) * jnp.roll(magnetic, -1, along)


def shards_general(section, start, velocity, pair_list, wavenumber):
    pair_count = pair_list.shape[0]
    leg_table, first_half, degree = pair_table(pair_list, NM, NLAT)
    legendre = leg_table.astype(jnp.bfloat16)
    selectors = jnp.stack([first_half, jnp.logical_not(first_half)], axis=1)
    masks_low = selectors.astype(jnp.bfloat16)
    anchor = (pair_list == 0)[:, None] & (jnp.arange(NM + 1) == 0)[None, :]
    anchor_rows = anchor.reshape(-1).astype(jnp.float32)
    part_pick = jnp.array([1.0, 0.0], jnp.float32)
    forcing = test_field(wavenumber[0], TESTS, LEV)
    spec_field = (
        section[0].astype(jnp.float32)
        + forcing[:, :, :, None, None] * part_pick[:, None] * anchor_rows[None, :]
    )
    spec_field = spec_field.astype(jnp.bfloat16).reshape(TESTS, 3, LEV, 2, pair_count, NM + 1)
    masked = spec_field[:, :, :, :, :, None, :] * masks_low
    spectra = jnp.einsum(
        "scvpqhr,rqa->ascvpqh", masked, legendre, preferred_element_type=jnp.float32
    )
    spectra = spectra.astype(jnp.bfloat16).reshape(NLAT, TESTS, 3, LEV, 2, 2 * pair_count)
    every_pair = lax.all_gather(pair_list, "ma", axis=0, tiled=True)
    order_list = jnp.stack([every_pair, NM - 1 - every_pair], axis=1).reshape(-1)
    waves = wave_table(order_list, NLON)
    inverse_table = (waves * grid_scale).astype(jnp.bfloat16)
    forward_table = (waves * (2.0 * jnp.pi / NLON)).astype(jnp.bfloat16)
    wind_field = lax.all_gather(velocity, "team", axis=2, tiled=True)
    band_size = velocity.shape[0]
    latitudes = lax.axis_index("ma") * band_size + jnp.arange(band_size, dtype=jnp.int32)
    weights = lat_weights(latitudes, NLAT)
    collected = []
    for test_id in range(TESTS):
        grid_field = jnp.einsum(
            "ascvpm,pmo->ascvo",
            lax.all_to_all(
                spectra[:, test_id : test_id + 1], "ma", split_axis=0, concat_axis=5, tiled=True
            ),
            inverse_table,
            preferred_element_type=jnp.float32,
        )
        emf = cross_field(wind_field[:, None], grid_field, 2).astype(jnp.bfloat16)
        fourier = jnp.einsum(
            "ascvo,pmo->ascvpm", emf, forward_table, preferred_element_type=jnp.float32
        )
        fourier = (fourier * weights[:, None, None, None, None, None]).astype(jnp.bfloat16)
        collected.append(lax.all_to_all(fourier, "ma", split_axis=5, concat_axis=0, tiled=True))
    returned = jnp.concatenate(collected, axis=1)
    returned = returned.reshape(NLAT, TESTS, 3, LEV, 2, pair_count, 2)
    project = jnp.einsum(
        "ascvpqh,rqa->scvpqhr", returned, legendre, preferred_element_type=jnp.float32
    )
    tendency = jnp.sum(project * selectors.astype(jnp.float32), axis=5).reshape(
        TESTS, 3, LEV, 2, -1
    )
    spread = (degree * (degree + 1)).astype(jnp.float32).reshape(-1)
    updated = start[0] + step_weight * (
        tendency - diffusion * spread * section[0].astype(jnp.float32)
    )
    return updated[None]


BF16 = jnp.bfloat16
F32 = jnp.float32
VMEM_CAP = 56 << 20
PAIR_ROWS = NM + 1
CHUNK_ROWS = 16
TABLE_PAIRS = 32
SLOTS = 16


def work(micros):
    return pl.CostEstimate(
        flops=int(micros * 1e9), transcendentals=0, bytes_accessed=int(micros * 1e6)
    )


def after(value, *others):
    return lax.optimization_barrier((value,) + others)[0]


def table_window(slots):
    return -(-(PAIR_ROWS + slots - 1) // 32) * 32


def swap_major(block):
    return jnp.swapaxes(block, 0, 1)


def table_kernel(upper, lower, first, second, seed_low, seed_high, cosine, _, out, *, lead):
    shape = seed_low.shape
    cosine_rows = jnp.broadcast_to(cosine[...], shape)
    first_step = first[...]
    second_step = second[...]
    low_value = seed_low[...]
    high_value = seed_high[...]

    def chunk(starting, index, state):
        latest, before = state
        scale_up = upper[index]
        scale_down = lower[index]
        produced = []
        for offset in range(CHUNK_ROWS):
            step = index * CHUNK_ROWS + offset
            current = (scale_up[:, offset : offset + 1] * cosine_rows) * latest - scale_down[
                :, offset : offset + 1
            ] * before
            current = jnp.where(second_step == step, high_value, current)
            if starting:
                current = jnp.where(first_step == step, low_value, current)
            produced.append(current)
            latest, before = current, latest
        rows = swap_major(jnp.stack(produced))
        out[:, pl.ds(pl.multiple_of(index * CHUNK_ROWS, CHUNK_ROWS), CHUNK_ROWS), :] = rows.astype(
            BF16
        )
        return latest, before

    blank = jnp.zeros(shape, F32)
    state = lax.fori_loop(0, lead, functools.partial(chunk, True), (blank, blank))
    lax.fori_loop(lead, out.shape[1] // CHUNK_ROWS, functools.partial(chunk, False), state)


def legendre_table(every_pair, slots, lats):
    pairs = every_pair.shape[0]
    window = table_window(slots)
    order_low = every_pair.astype(F32)
    order_high = (NM - 1 - every_pair).astype(F32)
    colatitude = jnp.pi * (lats.astype(F32) + 0.5) / NLAT
    seed_low = seed_values(order_low, NM, jnp.sin(colatitude))
    seed_high = seed_values(order_high, NM, jnp.sin(colatitude))
    slot = jnp.arange(pairs, dtype=jnp.int32) % slots
    row = jnp.arange(window, dtype=jnp.int32)[None, :] - slot[:, None]
    switch = NM - every_pair
    in_low = row < switch[:, None]
    degree = jnp.where(in_low, every_pair[:, None] + row, row - 1)
    order = jnp.where(in_low, order_low[:, None], order_high[:, None])
    real = degree.astype(F32)
    active = (real > order) & (row >= 0) & (row < PAIR_ROWS)
    divisor = jnp.where(active, real * real - order * order, 1.0)
    upper = jnp.sqrt(jnp.maximum(4.0 * real * real - 1.0, 0.0) / divisor)
    lower_num = ((real - 1.0) * (real - 1.0) - order * order) * (2.0 * real + 1.0)
    lower = jnp.sqrt(
        jnp.maximum(lower_num, 0.0) / (divisor * jnp.maximum(2.0 * real - 3.0, 1.0))
    )
    by_chunk = lambda values: jnp.swapaxes(
        jnp.where(active, values, 0.0).reshape(pairs, window // CHUNK_ROWS, CHUNK_ROWS), 0, 1
    )
    lanes = lats.shape[0]
    spread_out = lambda values: jnp.broadcast_to(values[:, None], (pairs, lanes))
    chunks = window // CHUNK_ROWS
    operands = (
        by_chunk(upper),
        by_chunk(lower),
        spread_out(slot),
        spread_out(slot + switch),
        seed_low,
        seed_high,
        jnp.cos(colatitude)[None, :],
    )
    blocks = pairs // TABLE_PAIRS
    shape = jax.ShapeDtypeStruct((pairs, window, lanes), BF16)
    halves = []
    for begin, end in ((0, blocks // 2), (blocks // 2, blocks)):
        place = lambda q, begin=begin: q + begin
        coefficient = pl.BlockSpec(
            (chunks, TABLE_PAIRS, CHUNK_ROWS), lambda q, place=place: (0, place(q), 0)
        )
        per_pair = pl.BlockSpec((TABLE_PAIRS, lanes), lambda q, place=place: (place(q), 0))
        before = halves[-1:] or [jnp.zeros((8, 128), BF16)]
        halves.append(
            pl.pallas_call(
                functools.partial(table_kernel, lead=-(-slots // CHUNK_ROWS)),
                grid=(end - begin,),
                in_specs=[coefficient, coefficient, per_pair, per_pair, per_pair, per_pair]
                + [pl.BlockSpec((1, lanes), lambda q: (0, 0))]
                + [pl.BlockSpec(memory_space=pl.ANY)],
                out_specs=pl.BlockSpec(
                    (TABLE_PAIRS, window, lanes), lambda q, place=place: (place(q), 0, 0)
                ),
                out_shape=shape,
                input_output_aliases={7: 0} if halves else {},
                compiler_params=pltpu.CompilerParams(vmem_limit_bytes=VMEM_CAP),
                cost_estimate=work(20),
                name="table",
            )(*operands, *before)
        )
    return halves


def row_mask(switch, source, place, slots, lane):
    turn = switch[source * slots + place]
    in_low = lane < turn
    even = ((lane - jnp.where(in_low, place, turn)) & 1) == 0
    anchor = (lane == place) & (turn == place + NM)
    return in_low, even, anchor


def mirror_sign(fields):
    lane = lax.broadcasted_iota(jnp.int32, (fields, 128), 1)
    return jnp.where(lane < 64, 1.0, -1.0).astype(F32)


def synthesis_kernel(switch, spec, table, forcing, out, *, slots):
    source = pl.program_id(0)
    window = table.shape[1]
    pieces = spec.shape[2]
    fields = 4 * pieces
    sign = mirror_sign(fields)
    lane = lax.broadcasted_iota(jnp.int32, (fields, window), 1)
    force = jnp.broadcast_to(forcing[...], (fields, window))

    def group(index, _):
        collected = []
        for slot in range(SLOTS):
            place = index * SLOTS + slot
            in_low, even, anchor = row_mask(switch, source, place, slots, lane)
            span = pl.ds(pl.multiple_of(place * NM, NM), window)
            rows = jnp.concatenate(
                [
                    spec[team, 0, piece, :, span].astype(F32)
                    for team in range(2)
                    for piece in range(pieces)
                ],
                axis=0,
            )
            rows = rows + jnp.where(anchor, force, 0.0)
            low, high = jnp.where(in_low, rows, 0.0), jnp.where(in_low, 0.0, rows)
            split = [
                jnp.where(even, low, 0.0),
                jnp.where(even, 0.0, low),
                jnp.where(even, high, 0.0),
                jnp.where(even, 0.0, high),
            ]
            made = jnp.dot(
                jnp.concatenate(split, axis=0).astype(BF16),
                table[place],
                preferred_element_type=F32,
            )
            for order in range(2):
                same = made[2 * order * fields : (2 * order + 1) * fields]
                flips = made[(2 * order + 1) * fields : (2 * order + 2) * fields]
                collected.append(
                    jnp.concatenate(
                        [
                            same[:, :128] + flips[:, :128],
                            same[:, :128] - flips[:, :128],
                            same[:, 128:] + sign * flips[:, 128:],
                        ],
                        axis=1,
                    )
                )
        rows = pl.ds(pl.multiple_of(index * 2 * SLOTS, 2 * SLOTS), 2 * SLOTS)
        out[:, rows, :] = swap_major(jnp.stack(collected)).astype(BF16)
        return 0

    lax.fori_loop(0, slots // SLOTS, group, 0)


def synthesis(spec, table, forcing, switch, slots):
    _, sources, pieces, parts, width = spec.shape
    fields = 2 * pieces * parts
    pairs, window, lanes = table.shape
    return pl.pallas_call(
        functools.partial(synthesis_kernel, slots=slots),
        grid_spec=pltpu.PrefetchScalarGridSpec(
            num_scalar_prefetch=1,
            grid=(sources,),
            in_specs=[
                pl.BlockSpec((2, 1, pieces, parts, width), lambda z, _: (0, z, 0, 0, 0)),
                pl.BlockSpec((slots, window, lanes), lambda z, _: (z, 0, 0)),
                pl.BlockSpec((fields, 1), lambda z, _: (0, 0)),
            ],
            out_specs=pl.BlockSpec((fields, 2 * slots, NLAT), lambda z, _: (0, z, 0)),
        ),
        out_shape=jax.ShapeDtypeStruct((fields, 2 * pairs, NLAT), BF16),
        compiler_params=pltpu.CompilerParams(vmem_limit_bytes=VMEM_CAP),
        cost_estimate=work(14),
        name="synthesis",
    )(switch, spec, table, forcing)


LON_TILE = 768


def grid_kernel(
    spectra, first, second, arrange, inverse_cos, inverse_sin, forward_cos, forward_sin, weights,
    out, wind, emf,
):
    @pl.when(pl.program_id(0) == 0)
    def _():
        for c in range(3):
            bands = [
                half[z, c] for z in range(first.shape[0]) for half in (first, second)
            ]
            wind[c] = lax.dot_general(
                jnp.concatenate(bands, axis=0),
                arrange[...],
                (((0,), (0,)), ((), ())),
                preferred_element_type=F32,
            ).astype(BF16)

    for tile in range(NLON // LON_TILE):
        span = pl.ds(tile * LON_TILE, LON_TILE)
        magnetic = [
            jnp.dot(inverse_cos[span, :], spectra[2 * c], preferred_element_type=F32)
            + jnp.dot(inverse_sin[span, :], spectra[2 * c + 1], preferred_element_type=F32)
            for c in range(3)
        ]
        motion = [wind[c, span, :].astype(F32) for c in range(3)]
        for c in range(3):
            one, two = (c + 1) % 3, (c + 2) % 3
            emf[c, span, :] = (
                motion[one] * magnetic[two] - motion[two] * magnetic[one]
            ).astype(BF16)
    scale = weights[...]
    for c in range(3):
        for part, table in enumerate((forward_cos, forward_sin)):
            back = jnp.dot(table[...], emf[c], preferred_element_type=F32)
            out[2 * c + part] = (back * scale).astype(BF16)


def grid_product(spectra, first, second, arrange, tables, weights):
    fields, orders, lats = spectra.shape
    whole = lambda array: pl.BlockSpec(array.shape, lambda g: (0,) * array.ndim)
    per_group = pl.BlockSpec((6, orders, lats), lambda g: (g, 0, 0))
    fixed = (first, second, arrange) + tuple(tables) + (weights,)
    return pl.pallas_call(
        grid_kernel,
        grid=(fields // 6,),
        in_specs=[per_group] + [whole(array) for array in fixed],
        out_specs=per_group,
        out_shape=jax.ShapeDtypeStruct(spectra.shape, BF16),
        scratch_shapes=[pltpu.VMEM((3, NLON, lats), BF16)] * 2,
        compiler_params=pltpu.CompilerParams(vmem_limit_bytes=VMEM_CAP),
        cost_estimate=work(16),
        name="grid_product",
    )(spectra, *fixed)


def analysis_kernel(switch, fourier, table, out, *, slots):
    source = pl.program_id(0)
    window = table.shape[1]
    fields = fourier.shape[0]
    pieces = out.shape[2]
    width = out.shape[4]
    sign = mirror_sign(fields)
    lane = lax.broadcasted_iota(jnp.int32, (fields, window), 1)
    blank = jnp.zeros((fields, 128 - (window - NM)), F32)

    def store(values, span):
        for team in range(2):
            for piece in range(pieces):
                row = 2 * (team * pieces + piece)
                out[team, 0, piece, :, span] = values[row : row + 2].astype(BF16)

    def group(index, over):
        rows = pl.ds(pl.multiple_of(index * 2 * SLOTS, 2 * SLOTS), 2 * SLOTS)
        by_order = swap_major(fourier[:, rows, :].astype(F32))
        for slot in range(SLOTS):
            place = index * SLOTS + slot
            in_low, even, _ = row_mask(switch, source, place, slots, lane)
            split = []
            for order in range(2):
                values = by_order[2 * slot + order]
                north, south, rest = values[:, :128], values[:, 128:256], values[:, 256:]
                split += [
                    jnp.concatenate([north + south, rest], axis=1),
                    jnp.concatenate([north - south, rest * sign], axis=1),
                ]
            made = lax.dot_general(
                jnp.concatenate(split, axis=0).astype(BF16),
                table[place],
                (((1,), (1,)), ((), ())),
                preferred_element_type=F32,
            )
            part = [made[k * fields : (k + 1) * fields] for k in range(4)]
            made = jnp.where(
                in_low, jnp.where(even, part[0], part[1]), jnp.where(even, part[2], part[3])
            )
            start = pl.multiple_of(place * NM, NM)
            store(
                jnp.concatenate([made[:, :128] + over, made[:, 128:NM]], axis=1),
                pl.ds(start, NM),
            )
            over = jnp.concatenate([made[:, NM:], blank], axis=1)
        return over

    over = lax.fori_loop(0, slots // SLOTS, group, jnp.zeros((fields, 128), F32))
    full = slots * NM
    store(over[:, : width - full], pl.ds(full, width - full))


def analysis(fourier, table, switch, slots, width):
    fields, orders, lats = fourier.shape
    pairs, window, lanes = table.shape
    sources = pairs // slots
    pieces = fields // 4
    return pl.pallas_call(
        functools.partial(analysis_kernel, slots=slots),
        grid_spec=pltpu.PrefetchScalarGridSpec(
            num_scalar_prefetch=1,
            grid=(sources,),
            in_specs=[
                pl.BlockSpec((fields, 2 * slots, NLAT), lambda z, _: (0, z, 0)),
                pl.BlockSpec((slots, window, lanes), lambda z, _: (z, 0, 0)),
            ],
            out_specs=pl.BlockSpec((2, 1, pieces, 2, width), lambda z, _: (0, z, 0, 0, 0)),
        ),
        out_shape=jax.ShapeDtypeStruct((2, sources, pieces, 2, width), BF16),
        compiler_params=pltpu.CompilerParams(vmem_limit_bytes=VMEM_CAP),
        cost_estimate=work(14),
        name="analysis",
    )(switch, fourier, table)


def pack_kernel(section, out):
    out[0] = section[:, 0, 0]


def pack_level(section, level):
    pieces, targets, _, parts, width = section.shape
    return pl.pallas_call(
        pack_kernel,
        grid=(targets,),
        in_specs=[pl.BlockSpec((pieces, 1, 1, parts, width), lambda d: (0, d, level, 0, 0))],
        out_specs=pl.BlockSpec((1, pieces, parts, width), lambda d: (d, 0, 0, 0)),
        out_shape=jax.ShapeDtypeStruct((targets, pieces, parts, width), BF16),
        cost_estimate=work(5),
        name="pack",
    )(section)


def finish_kernel(base, tendency, out):
    fields = tendency.shape[2]
    for field in range(fields):
        out[0, field, :, :, 0] = base[0, field, :, :, 0] + step_weight * tendency[
            :, :, field
        ].astype(F32)


def finish(total, tendency, level):
    tests, comps, teams, count, depth, parts, width = total.shape
    own = pl.BlockSpec(
        (1, comps, teams, count, 1, parts, width), lambda s: (s, 0, 0, 0, level, 0, 0)
    )
    return pl.pallas_call(
        finish_kernel,
        grid=(tests,),
        in_specs=[
            own,
            pl.BlockSpec((teams, count, comps, parts, width), lambda s: (0, 0, s, 0, 0)),
        ],
        out_specs=own,
        out_shape=jax.ShapeDtypeStruct(total.shape, F32),
        input_output_aliases={0: 0},
        compiler_params=pltpu.CompilerParams(vmem_limit_bytes=VMEM_CAP),
        cost_estimate=work(5),
        name="finish",
    )(total, tendency)


def gather_pairs(pair_list, count):
    own = pair_list.shape[0]
    place = lax.axis_index("ma")
    every = jnp.zeros((count, own), jnp.int32)
    every = lax.dynamic_update_slice(every, pair_list[None], (place, 0))
    for shift in range(1, count):
        moved = lax.ppermute(pair_list, "ma", [(k, (k + shift) % count) for k in range(count)])
        every = lax.dynamic_update_slice(every, moved[None], ((place - shift) % count, 0))
    return every.reshape(-1)


def shards_by_level(section, start, velocity, pair_list, wavenumber, *, count):
    slots = pair_list.shape[0]
    width = section.shape[-1]
    depth = LEV // (2 * count)
    band = velocity.shape[0]
    place = lax.axis_index("ma")
    across = lax.axis_index("x")
    core = lax.axis_index("k")
    swap_cores = [(0, 1), (1, 0)]
    by_level = section.reshape(TESTS * 3, 2 * count, depth, 2, width)
    sent = pack_level(by_level, 0)
    every_pair = gather_pairs(pair_list, count)
    slot_of = jnp.arange(count * slots, dtype=jnp.int32) % slots
    switch = slot_of + NM - every_pair

    other = lax.ppermute(wavenumber, "k", swap_cores)
    waves_here = jnp.where(core == 0, jnp.stack([wavenumber, other]), jnp.stack([other, wavenumber]))
    forcing = jnp.stack([test_field(waves_here[team, 0], TESTS, LEV) for team in range(2)])
    forcing = forcing.reshape(2 * TESTS * 3, LEV)
    forcing = lax.dynamic_slice_in_dim(forcing, (core * count + place) * depth, depth, axis=1)
    forcing = jnp.stack([forcing, jnp.zeros_like(forcing)], axis=1).reshape(-1, depth)

    exchange = functools.partial(
        lax.all_to_all, axis_name=("k", "ma"), split_axis=0, concat_axis=0, tiled=True
    )
    arrived = exchange(sent)
    specs = [arrived]

    side = count // 2
    bands = velocity.transpose(2, 1, 0, 3)
    pieces = []
    for turn in range(side):
        block = lax.dynamic_slice_in_dim(bands, (place + turn) % side * depth, depth, axis=0)
        route = [
            (
                sender * count + origin,
                origin // side * count + sender * side + (origin + turn) % side,
            )
            for sender in range(2)
            for origin in range(count)
        ]
        pieces.append(lax.ppermute(block, ("k", "ma"), route))

    mid = NLAT // 2
    north = jnp.arange(mid, dtype=jnp.int32)
    lats = jnp.concatenate(
        [north[:128], NLAT - 1 - north[:128], north[128:], NLAT - 1 - north[128:]]
    )
    shift = (place - jnp.arange(side, dtype=jnp.int32)) % side
    origin = side * jnp.stack([1 - across, across])[None, :] + shift[:, None]
    rows = band * origin[:, :, None] + jnp.arange(band, dtype=jnp.int32)
    arrange = (rows.reshape(-1)[:, None] == lats[None, :]).astype(BF16)
    half_table, table = legendre_table(every_pair, slots, jnp.concatenate([north, north[128:]]))
    order_list = jnp.stack([every_pair, NM - 1 - every_pair], axis=1).reshape(-1)
    waves = wave_table(order_list, NLON)
    inverse_table = (waves * grid_scale).astype(BF16)
    forward_table = (waves * (2.0 * jnp.pi / NLON)).astype(BF16)
    tables = (inverse_table[0].T, inverse_table[1].T, forward_table[0], forward_table[1])
    weights = lat_weights(lats, NLAT)[None, :]

    row_index = jnp.arange(PAIR_ROWS, dtype=jnp.int32)
    first_half = row_index[None, :] < (NM - pair_list)[:, None]
    degree = jnp.where(first_half, pair_list[:, None] + row_index[None, :], row_index[None, :] - 1)
    spread = (degree * (degree + 1)).astype(F32).reshape(-1)
    total = start[0] - (step_weight * diffusion) * spread * section[0].astype(F32)
    total = total.reshape(TESTS, 3, 2, count, depth, 2, width)

    winds = []
    last = (arrived,)
    for group in (slice(0, 1), slice(1, depth)):
        part = after(jnp.stack([piece[group] for piece in pieces], axis=1), *last)
        turn = lax.ppermute(part, ("x", "k"), [(0, 2), (1, 0), (2, 3), (3, 1)])
        cross = lax.ppermute(part, ("x", "k"), [(1, 2), (2, 1)])
        other = jnp.where(across == core, part, cross)
        winds += [(turn[k], other[k]) for k in range(turn.shape[0])]
        last = (turn, cross)

    first_spectra = synthesis(
        arrived.reshape(2, count, TESTS * 3, 2, width), table, forcing[:, :1], switch, slots
    )
    last = (arrived,)
    for level in range(1, depth):
        packed = pack_level(by_level, level)
        specs.append(exchange(after(packed, *last)))
        last = (specs[-1],)
    specs = [spec.reshape(2, count, TESTS * 3, 2, width) for spec in specs]

    for level in range(depth):
        spectra = first_spectra
        if level:
            spectra = synthesis(specs[level], table, forcing[:, level : level + 1], switch, slots)
        fourier = grid_product(spectra, *winds[level], arrange, tables, weights)
        tendency = analysis(fourier, table, switch, slots, width)
        back = exchange(after(tendency.reshape(2 * count, TESTS * 3, 2, width), *last))
        last = (back,)
        total = finish(total, back.reshape(2, count, TESTS * 3, 2, width), level)
    return total.reshape(start.shape)


def solution(mesh):
    sizes = dict(mesh.shape)
    count = sizes["ma"]
    whole_slots = (NM // 2) % (count * SLOTS) == 0
    if sizes["team"] == 4 and count % 2 == 0 and LEV % (2 * count) == 0 and whole_slots:
        grid = Mesh(
            mesh.devices.reshape(sizes["run"], 2, 2, count), ("run", "x", "k", "ma")
        )
        team = ("x", "k")
        body = lambda *arrays: shards_by_level(*arrays, count=count)
    else:
        grid, team, body = mesh, ("team",), shards_general
    placed = (
        P(("run",) + team, None, None, None, None, "ma"),
        P(("run",) + team, None, None, None, None, "ma"),
        P(("run", "ma"), None, team, None),
        P("ma"),
        P(team),
    )
    return jax.shard_map(
        body,
        mesh=grid,
        in_specs=placed,
        out_specs=P(("run",) + team, None, None, None, None, "ma"),
        check_vma=False,
    )
```
